256 devices in a mesh: tm: 8 (over x_lo, y), wall: 4 (over x_hi, core), span: 8 (over z).
Axes of the slice: x: 4 (x_hi: 2, x_lo: 2; x = x_hi * 2 + x_lo), y: 4, z: 8, core: 2. Of those that a mesh axis runs over, the one named last changes fastest.
Arguments:
- starting_speed_vector: float32 [3, 8, 16, 128, 1024], P(None, 'tm', None, 'wall', 'span'), may hold values from -6 to 6
- driving_source: float32 [3, 8, 16, 128, 1024], P(None, 'tm', None, 'wall', 'span'), may hold values from -3 to 3
- viscosity: float32 [128], P('wall'), may hold values from 0.02 to 0.2
Outputs:
- orbit: float32 [3, 8, 16, 128, 1024], P(None, 'tm', None, 'wall', 'span')
- residual: float32 [3, 8, 16, 128, 1024], P(None, 'tm', None, 'wall', 'span')
The draws below stay inside these ranges and needn't reach their ends.
All inputs are finite; a program needn't handle non-finite values.
Results may differ from the reference program's by a relative error of at most 0.0001.
Values sent between devices are 32-bit elements; how exact they have to be, the bound alone decides.
A program may use at most 64 MiB of HBM per device.

```python
import math
import jax
import jax.numpy as jnp

LENGTHWISE_SLABS = 16
ITERS = 2
TIME_LEVELS = 8
NORMAL_LAYERS = 128
CROSSWISE_POINTS = 1024


def steps_of(stream_key, dims, cuts, smallest, largest):
    def one(position, parts):
        heights = jax.random.uniform(jax.random.fold_in(jax.random.fold_in(stream_key, 6), position), (parts,), jnp.float32, smallest / len(cuts), largest / len(cuts))
        return jnp.repeat(jnp.exp(heights), dims[position] // parts).reshape((-1,) + (1,) * (len(dims) - position - 1))

    factor_of = one(*cuts[0])
    for cut in cuts[1:]:
        factor_of = factor_of * one(*cut)
    return factor_of


def noise(key, shape, deviation, reach, cuts=(), kind=jnp.bfloat16):
    entries = deviation * jax.random.normal(key, shape, jnp.float32)
    if cuts:
        entries = entries * steps_of(key, shape, cuts, -0.22, 0.18)
    return jnp.clip(entries, -reach, reach).astype(kind)


def setup_inputs(seed: int = 0) -> dict:
    splits = jax.random.split(jax.random.key(seed), 4)
    return {
        "starting_speed_vector": noise(splits[0], (3, TIME_LEVELS, LENGTHWISE_SLABS, NORMAL_LAYERS, CROSSWISE_POINTS), 1.0, 6.0, ((1, 8), (3, 4), (4, 8)), jnp.float32),
        "driving_source": noise(splits[1], (3, TIME_LEVELS, LENGTHWISE_SLABS, NORMAL_LAYERS, CROSSWISE_POINTS), 0.5, 3.0, ((1, 8), (3, 4), (4, 8)), jnp.float32),
        "viscosity": jnp.clip(jnp.exp(math.log(0.2) - 2.3025851 * jax.random.uniform(splits[2], (NORMAL_LAYERS,), jnp.float32) ** steps_of(splits[2], (NORMAL_LAYERS,), ((0, 4),), -0.2, 0.2)), 0.02, 0.2),
    }


step_rate = 0.05


def forward_cell(values, axis):
    if axis == 3:
        zeros_row = jnp.zeros_like(values[:, :, :, :1])
        return jnp.concatenate((values[:, :, :, 1:], zeros_row), 3)
    return jnp.roll(values, -1, axis)


def backward_cell(values, axis):
    if axis == 3:
        zeros_row = jnp.zeros_like(values[:, :, :, :1])
        return jnp.concatenate((zeros_row, values[:, :, :, :-1]), 3)
    return jnp.roll(values, 1, axis)


def central(values, axis):
    return 0.5 * (forward_cell(values, axis) - backward_cell(values, axis))


def laplacian(values):
    total = forward_cell(values, 2) + backward_cell(values, 2) - 2.0 * values
    total = total + (forward_cell(values, 3) + backward_cell(values, 3) - 2.0 * values)
    return total + (forward_cell(values, 4) + backward_cell(values, 4) - 2.0 * values)


def reflect(values):
    midperiod_translation = TIME_LEVELS // 2
    turned = jnp.roll(values, -midperiod_translation, 1)[:, :, :, ::-1, :]
    sign_row = jnp.array([1.0, -1.0, 1.0], dtype=jnp.float32).reshape(3, 1, 1, 1, 1)
    return turned * sign_row


def reference(starting_speed_vector, driving_source, viscosity):
    viscous = viscosity[None, None, None, :, None]
    present_state = starting_speed_vector
    residual = starting_speed_vector
    for iteration in range(ITERS):
        slopes = [central(present_state, 2 + axis_id) for axis_id in range(3)]
        advect = present_state[0:1] * slopes[0] + present_state[1:2] * slopes[1] + present_state[2:3] * slopes[2]
        residual = (0.5 * (jnp.roll(present_state, -1, 1) - jnp.roll(present_state, 1, 1)) + advect
                    - viscous * laplacian(present_state) + 0.5 * (present_state - reflect(present_state)) - driving_source)
        transport = jnp.stack([jnp.sum(residual * slopes[component], axis=0) for component in range(3)])
        second = (central(present_state[0:1] * residual, 2) + central(present_state[1:2] * residual, 3)
                  + central(present_state[2:3] * residual, 4))
        descent = (-0.5 * (jnp.roll(residual, -1, 1) - jnp.roll(residual, 1, 1)) + transport - second
                   - laplacian(viscous * residual) + 0.5 * (residual - reflect(residual)))
        present_state = present_state - step_rate * descent
    return present_state, residual
```

```python
import jax
import jax.numpy as jnp
from jax import lax
from jax.experimental import pallas as pl
from jax.experimental.pallas import tpu as pltpu
from jax.sharding import PartitionSpec as P

STEP = 0.05
SIGN = (1.0, -1.0, 1.0)
MESH = pl.DeviceIdType.MESH
OFFSETS = [(dx, dy) for dx in range(4) for dy in range(4) if (dx, dy) != (0, 0)]
ROW0 = 8


def roll(v, shift, axis=1):
    return pltpu.roll(v, shift % 128 if isinstance(shift, int) else shift, axis)


def device_of(x, y, cls, z):
    xh, xl = x // 2, lax.rem(x, 2)
    return (xl * 4 + y, xh * 2 + (cls + xh - 2 * cls * xh), z)


def position():
    tm, wall, z = lax.axis_index("tm"), lax.axis_index("wall"), lax.axis_index("span")
    xl, y, xh, core = tm // 4, lax.rem(tm, 4), wall // 2, lax.rem(wall, 2)
    return xh * 2 + xl, y, core + xh - 2 * core * xh, z


def path_of(x, y):
    odd = lax.rem(y, 2)
    return 4 * y + x + odd * (3 - 2 * x)


def chip_at(p):
    y, a = p // 4, lax.rem(p, 4)
    odd = lax.rem(y, 2)
    return a + odd * (3 - 2 * a), y


def group_of(p, z):
    return p + lax.rem(z, 2) * (15 - 2 * p)


def slot_of(x, y):
    xh, xl = x // 2, lax.rem(x, 2)
    return xh, lax.rem(4 * xl + y + 4 * xh, 8)


def along_path(p, z, way):
    there = p + way * (1 - 2 * lax.rem(z, 2))
    over = (there + 16) // 16 - 1
    over = over * over
    x, y = chip_at(there * (1 - over) + p * over)
    return x, y, lax.rem(z + way * over + 8, 8)


def swap_groups(ins):
    lane = lax.broadcasted_iota(jnp.int32, (8, 128), 1)
    turned = [roll(v, 8 * i) for i, v in enumerate(ins)]
    mixed = [turned[-d % 16] for d in range(16)]
    for bit in range(4):
        mask = (lane & (8 << bit)) != 0
        mixed = [jnp.where(mask, mixed[(d - (1 << bit)) % 16], mixed[d]) for d in range(16)]
    return [roll(v, -8 * d) for d, v in enumerate(mixed)]


def frame_rows(v, xh):
    row = lax.broadcasted_iota(jnp.int32, (8, 128), 0)
    return jnp.take_along_axis(v, row + xh * (7 - 2 * row), axis=0, mode="promise_in_bounds")


def frame_sign(c, xh):
    xf = xh.astype(jnp.float32)
    return 1.0 - 2.0 * xf if SIGN[c] < 0 else None


def pack(src, dst, xh):
    def one(step, _):
        t = step
        to = t + xh * (3 - 2 * t)
        for c in range(3):
            sign = frame_sign(c, xh)
            ins = [src[c, i, pl.ds(pl.multiple_of(8 * t, 8), 8), :] for i in range(16)]
            for d, v in enumerate(swap_groups(ins)):
                v = frame_rows(v, xh)
                v = v if sign is None else v * sign
                dst[d, c, pl.ds(pl.multiple_of(8 * to, 8), 8), :] = v
        return 0

    lax.fori_loop(0, 4, one, 0)


def unpack(src, dst, xh):
    def one(step, _):
        t = step
        to = t + xh * (3 - 2 * t)
        for c in range(3):
            sign = frame_sign(c, xh)
            ins = [src[d, c, pl.ds(pl.multiple_of(8 * to, 8), 8), :] for d in range(16)]
            for i, v in enumerate(swap_groups(ins)):
                v = frame_rows(v, xh)
                v = v if sign is None else v * sign
                dst[c, i, pl.ds(pl.multiple_of(8 * t, 8), 8), :] = v
        return 0

    lax.fori_loop(0, 4, one, 0)


def pack_cells(field, left, right):
    cell = lax.broadcasted_iota(jnp.int32, (8, 128), 1) & 7

    def one(step, _):
        f, c = step // 3, lax.rem(step, 3)
        for t in range(4):
            lo = hi = None
            for n in range(8):
                v = field[f, n, c, ROW0 + 8 * t : ROW0 + 8 * t + 8, :]
                a, b = roll(v, n), roll(v, n - 7)
                lo = a if n == 0 else jnp.where(cell == n, a, lo)
                hi = b if n == 0 else jnp.where(cell == n, b, hi)
            left[f, c, 8 * t : 8 * t + 8, :] = lo
            right[f, c, 8 * t : 8 * t + 8, :] = hi
        return 0

    lax.fori_loop(0, 6, one, 0)


def pack_rows(field, edge, cls):
    def one(step, _):
        f, n = step // 8, lax.rem(step, 8)
        for c in range(3):
            first = field[f, n, c, ROW0 : ROW0 + 1, :]
            last = field[f, n, c, ROW0 + 31 : ROW0 + 32, :]
            edge[f, n, c : c + 1, :] = jnp.where(cls == 1, first, last)
        return 0

    lax.fori_loop(0, 16, one, 0)


def fill_rows(field, edge, cls):
    def one(step, _):
        f, n = step // 8, lax.rem(step, 8)
        for c in range(3):
            got = edge[f, n, c : c + 1, :]
            fold = SIGN[c] * field[1 - f, lax.rem(n + 4, 8), c, ROW0 + 31 : ROW0 + 32, :]
            field[f, n, c, ROW0 - 1 : ROW0, :] = jnp.where(cls == 1, got, 0.0)
            field[f, n, c, ROW0 + 32 : ROW0 + 33, :] = jnp.where(cls == 1, fold, got)
        return 0

    lax.fori_loop(0, 16, one, 0)


def shifts(field, left, right, f, n, c, t, cell):
    r0 = ROW0 + 8 * t
    v = field[f, n, c, r0 : r0 + 8, :]
    edge_hi = right[f, c, 8 * t : 8 * t + 8, :]
    edge_lo = left[f, c, 8 * t : 8 * t + 8, :]
    plane = (roll(v, -8), roll(v, 8))
    row = (field[f, n, c, r0 + 1 : r0 + 9, :], field[f, n, c, r0 - 1 : r0 + 7, :])
    span = (
        jnp.where(cell == 7, roll(edge_hi, 7 - n), roll(v, -1)),
        jnp.where(cell == 0, roll(edge_lo, lax.rem(128 - n, 128)), roll(v, 1)),
    )
    return v, plane, row, span


def residual_stage(field, left, right, nu, force, slopes, out):
    cell = lax.broadcasted_iota(jnp.int32, (8, 128), 1) & 7

    def one(step, _):
        f, n = step // 8, lax.rem(step, 8)
        ahead, behind = lax.rem(n + 1, 8), lax.rem(n + 7, 8)
        for t in range(4):
            r0 = ROW0 + 8 * t
            rows = slice(r0, r0 + 8)
            centre, slope, laps = [], [], []
            for c in range(3):
                v, plane, row, span = shifts(field, left, right, f, n, c, t, cell)
                d = [0.5 * (a - b) for a, b in (plane, row, span)]
                for axis in range(3):
                    slopes[f, n, axis, c, 8 * t : 8 * t + 8, :] = d[axis]
                lap = (plane[0] + plane[1]) + (row[0] + row[1]) + (span[0] + span[1]) - 6.0 * v
                centre.append(v)
                slope.append(d)
                laps.append(lap)
            mu = nu[f, rows, :]
            for c in range(3):
                s = slope[c]
                advect = centre[0] * s[0] + centre[1] * s[1] + centre[2] * s[2]
                drift = field[f, ahead, c, rows, :] - field[f, behind, c, rows, :]
                pull = centre[c] - field[1 - f, n, c, rows, :]
                value = 0.5 * (drift + pull) + advect - mu * laps[c]
                if force is not None:
                    value = value - force[f, n, c, 8 * t : 8 * t + 8, :]
                out[f, n, c, rows, :] = value
        return 0

    lax.fori_loop(0, 16, one, 0)


def subtract_stage(out, force):
    def one(step, _):
        f, n = step // 8, lax.rem(step, 8)
        for c in range(3):
            out[f, n, c, ROW0 : ROW0 + 32, :] = out[f, n, c, ROW0 : ROW0 + 32, :] - force[f, n, c]
        return 0

    lax.fori_loop(0, 16, one, 0)


def descent_stage(field, left, right, res, res_left, res_right, nu, slopes, out):
    cell = lax.broadcasted_iota(jnp.int32, (8, 128), 1) & 7

    def one(step, _):
        f, n = step // 8, lax.rem(step, 8)
        ahead, behind = lax.rem(n + 1, 8), lax.rem(n + 7, 8)
        for t in range(4):
            r0 = ROW0 + 8 * t
            rows = slice(r0, r0 + 8)
            mu, mu_up, mu_down = nu[f, rows, :], nu[f, r0 + 1 : r0 + 9, :], nu[f, r0 - 1 : r0 + 7, :]
            u0 = field[f, n, 0, rows, :]
            u2 = field[f, n, 2, rows, :]
            up0, um0 = roll(u0, -8), roll(u0, 8)
            up1, um1 = field[f, n, 1, r0 + 1 : r0 + 9, :], field[f, n, 1, r0 - 1 : r0 + 7, :]
            edge_hi = right[f, 2, 8 * t : 8 * t + 8, :]
            edge_lo = left[f, 2, 8 * t : 8 * t + 8, :]
            up2 = jnp.where(cell == 7, roll(edge_hi, 7 - n), roll(u2, -1))
            um2 = jnp.where(cell == 0, roll(edge_lo, lax.rem(128 - n, 128)), roll(u2, 1))
            every = [shifts(res, res_left, res_right, f, n, c, t, cell) for c in range(3)]
            for c in range(3):
                r, plane, row, span = every[c]
                transport = None
                for e in range(3):
                    term = every[e][0] * slopes[f, n, c, e, 8 * t : 8 * t + 8, :]
                    transport = term if transport is None else transport + term
                second = (up0 * plane[0] - um0 * plane[1]) + (up1 * row[0] - um1 * row[1])
                second = second + (up2 * span[0] - um2 * span[1])
                diffused = mu * ((plane[0] + plane[1]) + (span[0] + span[1]) - 6.0 * r)
                diffused = diffused + (mu_up * row[0] + mu_down * row[1])
                drift = res[f, behind, c, rows, :] - res[f, ahead, c, rows, :]
                pull = r - res[1 - f, n, c, rows, :]
                descent = 0.5 * (drift + pull - second) + transport - diffused
                out[f, n, c, rows, :] = field[f, n, c, rows, :] - STEP * descent
        return 0

    lax.fori_loop(0, 16, one, 0)


def kernel(
    u_hbm, f_hbm, nu_in, out_r, out_u,
    raw_u, raw_f, pack_u, pack_f, field_a, field_b, force, res, slopes, nu,
    cells_out, cells_in, rows_out, rows_in,
    load_sem, self_sem, u_send, u_recv, f_send, f_recv, r_send, r_recv, o_send, o_recv,
    halo_send, halo_recv, nu_send, nu_recv,
):
    x, y, cls, z = position()
    xh = x // 2
    p = path_of(x, y)
    group = group_of(p, z)
    my_f, my_n = slot_of(x, y)
    rows = pl.ds(ROW0, 32)

    load_u = pltpu.make_async_copy(u_hbm, raw_u, load_sem.at[0])
    load_u.start()
    load_f = pltpu.make_async_copy(f_hbm, raw_f, load_sem.at[1])
    load_f.start()

    barrier = pltpu.get_barrier_semaphore()
    peers = [(lax.rem(x + dx, 4), lax.rem(y + dy, 4)) for dx, dy in OFFSETS]
    for px, py in peers:
        pl.semaphore_signal(barrier, inc=1, device_id=device_of(px, py, cls, z), device_id_type=MESH)
    for there in (
        device_of(x, y, 1 - cls, z),
        device_of(x, y, cls, lax.rem(z + 1, 8)),
        device_of(x, y, cls, lax.rem(z + 7, 8)),
    ):
        pl.semaphore_signal(barrier, inc=1, device_id=there, device_id_type=MESH)

    row_id = lax.broadcasted_iota(jnp.int32, (8, 128), 0)
    for t in range(4):
        tile = jnp.zeros((8, 128), jnp.float32)
        for s in range(8):
            r = 8 * t + s
            tile = jnp.where(row_id == s, nu_in[r + xh * (31 - 2 * r)], tile)
        nu[xh, ROW0 + 8 * t : ROW0 + 8 * t + 8, :] = tile

    load_u.wait()
    pack(raw_u, pack_u, xh)
    pl.semaphore_wait(barrier, len(OFFSETS) + 3)

    def remote(src, dst, send, recv, there):
        return pltpu.make_async_remote_copy(
            src_ref=src, dst_ref=dst, send_sem=send, recv_sem=recv, device_id=there, device_id_type=MESH
        )

    pending = []
    u_in = []
    for j, (px, py) in enumerate(peers):
        copy = remote(
            pack_u.at[group_of(path_of(px, py), z)], field_a.at[my_f, my_n, :, rows],
            u_send.at[j], u_recv.at[j], device_of(px, py, cls, z),
        )
        copy.start()
        u_in.append(copy)
    own_u = pltpu.make_async_copy(pack_u.at[group], field_a.at[my_f, my_n, :, rows], self_sem.at[0])
    own_u.start()
    nu_copy = remote(nu.at[xh, rows], nu.at[xh, rows], nu_send, nu_recv, device_of(3 - x, y, cls, z))
    nu_copy.start()
    pending += u_in

    load_f.wait()
    pack(raw_f, pack_f, xh)
    f_in = []

    def send_force(c):
        for j, (px, py) in enumerate(peers):
            copy = remote(
                pack_f.at[group_of(path_of(px, py), z), c], force.at[my_f, my_n, c],
                f_send.at[c, j], f_recv.at[c, j], device_of(px, py, cls, z),
            )
            copy.start()
            f_in.append(copy)

    own_f = pltpu.make_async_copy(pack_f.at[group], force.at[my_f, my_n], self_sem.at[1])
    own_f.start()
    send_force(0)
    send_force(1)

    nx, ny, nz = along_path(p, z, 1)
    bx, by, bz = along_path(p, z, -1)
    ahead_dev, behind_dev = device_of(nx, ny, cls, nz), device_of(bx, by, cls, bz)
    other_core = device_of(x, y, 1 - cls, z)

    def send_halos(k, values):
        pack_cells(values, cells_out.at[k, 0], cells_out.at[k, 1])
        sends = [
            remote(cells_out.at[k, 0], cells_in.at[k, 1], halo_send.at[k, 0], halo_recv.at[k, 0], behind_dev),
            remote(cells_out.at[k, 1], cells_in.at[k, 0], halo_send.at[k, 1], halo_recv.at[k, 1], ahead_dev),
        ]
        for copy in sends:
            copy.start()
        pack_rows(values, rows_out.at[k], cls)
        if k == 0:
            for f in range(2):
                edge = jnp.where(cls == 1, nu[f, ROW0 : ROW0 + 1, :], nu[f, ROW0 + 31 : ROW0 + 32, :])
                rows_out[k, f, 0, 3:4, :] = edge
        sends.append(
            remote(rows_out.at[k], rows_in.at[k], halo_send.at[k, 2], halo_recv.at[k, 2], other_core)
        )
        sends[-1].start()
        pending.extend(sends)
        return sends

    def take_halos(k, values, sends):
        sends[2].wait_recv()
        fill_rows(values, rows_in.at[k], cls)
        if k == 0:
            for f in range(2):
                got = rows_in[k, f, 0, 3:4, :]
                fold = nu[1 - f, ROW0 + 31 : ROW0 + 32, :]
                nu[f, ROW0 - 1 : ROW0, :] = jnp.where(cls == 1, got, 0.0)
                nu[f, ROW0 + 32 : ROW0 + 33, :] = jnp.where(cls == 1, fold, got)
        sends[0].wait_recv()
        sends[1].wait_recv()

    nu_copy.wait()
    own_u.wait()
    for copy in u_in:
        copy.wait_recv()

    sends = send_halos(0, field_a)
    send_force(2)
    take_halos(0, field_a, sends)
    residual_stage(field_a, cells_in.at[0, 0], cells_in.at[0, 1], nu, None, slopes, res)
    own_f.wait()
    for copy in f_in:
        copy.wait_recv()
    pending += f_in
    subtract_stage(res, force)

    sends = send_halos(1, res)
    take_halos(1, res, sends)
    descent_stage(
        field_a, cells_in.at[0, 0], cells_in.at[0, 1], res, cells_in.at[1, 0], cells_in.at[1, 1],
        nu, slopes, field_b,
    )
    sends = send_halos(2, field_b)
    take_halos(2, field_b, sends)
    residual_stage(field_b, cells_in.at[2, 0], cells_in.at[2, 1], nu, force, slopes, res)
    sends = send_halos(3, res)

    def send_back(values, dst, send, recv):
        copies = []
        for j, (px, py) in enumerate(peers):
            f, n = slot_of(px, py)
            copy = remote(
                values.at[f, n, :, rows], dst.at[group], send.at[j], recv.at[j], device_of(px, py, cls, z)
            )
            copy.start()
            copies.append(copy)
        return copies

    r_out = send_back(res, out_r, r_send, r_recv)
    own_r = pltpu.make_async_copy(res.at[my_f, my_n, :, rows], out_r.at[group], self_sem.at[2])
    own_r.start()
    take_halos(3, res, sends)
    descent_stage(
        field_b, cells_in.at[2, 0], cells_in.at[2, 1], res, cells_in.at[3, 0], cells_in.at[3, 1],
        nu, slopes, field_a,
    )
    o_out = send_back(field_a, out_u, o_send, o_recv)
    own_o = pltpu.make_async_copy(field_a.at[my_f, my_n, :, rows], out_u.at[group], self_sem.at[3])
    own_o.start()
    own_r.wait()
    own_o.wait()
    for copy in pending:
        copy.wait_send()
    for copy in r_out + o_out:
        copy.wait()


def finish(r_in, u_in, u_out, r_out):
    x, _, _, _ = position()
    unpack(u_in, u_out, x // 2)
    unpack(r_in, r_out, x // 2)


def local(starting_speed_vector, driving_source, viscosity):
    block = starting_speed_vector.shape
    flat = (3, 16, 32, 128)
    f32 = jnp.float32
    packed = jax.ShapeDtypeStruct((16, 3, 32, 128), f32)
    dma = pltpu.SemaphoreType.DMA
    padded = pltpu.VMEM((2, 8, 3, 48, 128), f32)
    got_r, got_u = pl.pallas_call(
        kernel,
        out_shape=(packed, packed),
        in_specs=[
            pl.BlockSpec(memory_space=pl.ANY),
            pl.BlockSpec(memory_space=pl.ANY),
            pl.BlockSpec(memory_space=pltpu.SMEM),
        ],
        out_specs=(pl.BlockSpec(memory_space=pl.ANY),) * 2,
        scratch_shapes=[
            pltpu.VMEM(flat, f32),
            pltpu.VMEM(flat, f32),
            pltpu.VMEM((16, 3, 32, 128), f32),
            pltpu.VMEM((16, 3, 32, 128), f32),
            padded,
            padded,
            pltpu.VMEM((2, 8, 3, 32, 128), f32),
            padded,
            pltpu.VMEM((2, 8, 3, 3, 32, 128), f32),
            pltpu.VMEM((2, 48, 128), f32),
            pltpu.VMEM((4, 2, 2, 3, 32, 128), f32),
            pltpu.VMEM((4, 2, 2, 3, 32, 128), f32),
            pltpu.VMEM((4, 2, 8, 8, 128), f32),
            pltpu.VMEM((4, 2, 8, 8, 128), f32),
            dma((2,)), dma((4,)),
            dma((15,)), dma((15,)), dma((3, 15)), dma((3, 15)),
            dma((15,)), dma((15,)), dma((15,)), dma((15,)),
            dma((4, 3)), dma((4, 3)), dma(()), dma(()),
        ],
        compiler_params=pltpu.CompilerParams(
            collective_id=0, has_side_effects=True, vmem_limit_bytes=48 * 1024 * 1024
        ),
        name="descend",
    )(starting_speed_vector.reshape(flat), driving_source.reshape(flat), viscosity)
    orbit, residual = pl.pallas_call(
        finish,
        out_shape=(jax.ShapeDtypeStruct(flat, f32), jax.ShapeDtypeStruct(flat, f32)),
        in_specs=[pl.BlockSpec(memory_space=pltpu.VMEM)] * 2,
        out_specs=(pl.BlockSpec(memory_space=pltpu.VMEM),) * 2,
        name="finish",
    )(got_r, got_u)
    return orbit.reshape(block), residual.reshape(block)


def solution(mesh):
    spec = P(None, "tm", None, "wall", "span")
    return jax.shard_map(
        local, mesh=mesh, in_specs=(spec, spec, P("wall")), out_specs=(spec, spec), check_vma=False
    )
```

```python
import jax
import jax.numpy as jnp
from jax import lax
from jax.experimental import pallas as pl
from jax.experimental.pallas import tpu as pltpu
from jax.sharding import PartitionSpec as P

STEP = 0.05
SIGN = (1.0, -1.0, 1.0)
MESH = pl.DeviceIdType.MESH
OFFSETS = [(dx, dy) for dx in range(4) for dy in range(4) if (dx, dy) != (0, 0)]
ROW0 = 8


def roll(v, shift, axis=1):
    return pltpu.roll(v, shift % 128 if isinstance(shift, int) else shift, axis)


def device_of(x, y, cls, z):
    xh, xl = x // 2, lax.rem(x, 2)
    return (xl * 4 + y, xh * 2 + (cls + xh - 2 * cls * xh), z)


def position():
    tm, wall, z = lax.axis_index("tm"), lax.axis_index("wall"), lax.axis_index("span")
    xl, y, xh, core = tm // 4, lax.rem(tm, 4), wall // 2, lax.rem(wall, 2)
    return xh * 2 + xl, y, core + xh - 2 * core * xh, z


def path_of(x, y):
    odd = lax.rem(y, 2)
    return 4 * y + x + odd * (3 - 2 * x)


def chip_at(p):
    y, a = p // 4, lax.rem(p, 4)
    odd = lax.rem(y, 2)
    return a + odd * (3 - 2 * a), y


def group_of(p, z):
    return p + lax.rem(z, 2) * (15 - 2 * p)


def slot_of(x, y):
    xh, xl = x // 2, lax.rem(x, 2)
    return xh, lax.rem(4 * xl + y + 4 * xh, 8)


def along_path(p, z, way):
    there = p + way * (1 - 2 * lax.rem(z, 2))
    over = (there + 16) // 16 - 1
    over = over * over
    x, y = chip_at(there * (1 - over) + p * over)
    return x, y, lax.rem(z + way * over + 8, 8)


def swap_groups(ins, before=0, after=0):
    lane = lax.broadcasted_iota(jnp.int32, (8, 128), 1)
    turned = [roll(v, lax.rem(8 * i + before + 128, 128)) for i, v in enumerate(ins)]
    mixed = [turned[-d % 16] for d in range(16)]
    for bit in range(4):
        mask = (lane & (8 << bit)) != 0
        mixed = [jnp.where(mask, mixed[(d - (1 << bit)) % 16], mixed[d]) for d in range(16)]
    return [roll(v, lax.rem(128 - 8 * d + after, 128)) for d, v in enumerate(mixed)]


def frame_rows(v, xh):
    row = lax.broadcasted_iota(jnp.int32, (8, 128), 0)
    return jnp.take_along_axis(v, row + xh * (7 - 2 * row), axis=0, mode="promise_in_bounds")


def frame_sign(v, c, xh):
    return v * (1.0 - 2.0 * xh.astype(jnp.float32)) if SIGN[c] < 0 else v


def tile(t):
    return pl.ds(pl.multiple_of(8 * t, 8), 8)


def pack(src, dst, xh, n):
    def one(t, _):
        to = tile(t + xh * (3 - 2 * t))
        for c in range(3):
            ins = [src[c, i, tile(t), :] for i in range(16)]
            for d, v in enumerate(swap_groups(ins, 0, n)):
                dst[d, c, to, :] = frame_sign(frame_rows(v, xh), c, xh)
        return 0

    lax.fori_loop(0, 4, one, 0)


def unpack_rows(src, dst, xh, n, t):
    to = tile(t + xh * (3 - 2 * t))
    for c in range(3):
        ins = [src[d, c, to, :] for d in range(16)]
        for i, v in enumerate(swap_groups(ins, -n, 0)):
            dst[c, i, tile(t), :] = frame_sign(frame_rows(v, xh), c, xh)


def unpack(src, dst, xh, n):
    def one(t, _):
        unpack_rows(src, dst, xh, n, t)
        return 0

    lax.fori_loop(0, 4, one, 0)


def residues():
    lane = lax.broadcasted_iota(jnp.int32, (8, 128), 1) & 7
    return [lane == q for q in range(8)]


class Edges:
    def __init__(self):
        self.first = self.last = None

    def add(self, masks, n, v):
        self.first = v if n == 0 else jnp.where(masks[n], v, self.first)
        self.last = v if n == 0 else jnp.where(masks[(n + 7) % 8], v, self.last)

    def store(self, out, f, c, t):
        out[f, 0, c, tile(t), :] = roll(self.first, 7)
        out[f, 1, c, tile(t), :] = roll(self.last, -7)


def pack_cells(field, out, f):
    masks = residues()

    def one(t, _):
        for c in range(3):
            edges = Edges()
            for n in range(8):
                edges.add(masks, n, field[f, n, c, tile(t + 1), :])
            edges.store(out, f, c, t)
        return 0

    lax.fori_loop(0, 4, one, 0)


def pack_rows(field, edge, final, cls):
    for f in range(2):
        for n in range(8):
            for c in range(3):
                first = field[f, n, c, ROW0 : ROW0 + 1, :]
                last = field[f, n, c, ROW0 + 31 : ROW0 + 32, :]
                edge[f, n, c : c + 1, :] = jnp.where(cls == 1, first, last)
                final[f, n, c : c + 1, :] = last


def fill_rows(field, edge, final, cls):
    row = lax.broadcasted_iota(jnp.int32, (8, 128), 0)
    sign = jnp.where(row == 1, SIGN[1], 1.0)
    for f in range(2):
        for n in range(8):
            got = edge[f, n]
            fold = sign * roll(final[1 - f, (n + 4) % 8], -4 if n < 4 else 4)
            low = jnp.where(cls == 1, got, 0.0)
            high = jnp.where(cls == 1, fold, got)
            for c in range(3):
                field[f, n, c, ROW0 - 1 : ROW0, :] = low[c : c + 1, :]
                field[f, n, c, ROW0 + 32 : ROW0 + 33, :] = high[c : c + 1, :]


def rotate_all(field, turned, wrap):
    def one(f, _):
        for c in range(3):
            for t in range(4):
                rows, out = slice(ROW0 + 8 * t, ROW0 + 8 * t + 8), slice(8 * t, 8 * t + 8)
                for n in range(8):
                    v = field[f, n, c, rows, :]
                    for kind, shift in enumerate((-8, 8, -1, 1)):
                        turned[kind, f, n, c, out, :] = roll(v, shift)
                    if n == 0:
                        wrap[0, f, c, out, :] = roll(v, 7)
                    if n == 7:
                        wrap[1, f, c, out, :] = roll(v, -7)
        return 0

    lax.fori_loop(0, 2, one, 0)


def times(turned, wrap, f, n, c, rows):
    ahead = wrap[0, f, c, rows, :] if n == 7 else turned[2, f, n + 1, c, rows, :]
    behind = wrap[1, f, c, rows, :] if n == 0 else turned[3, f, n - 1, c, rows, :]
    return ahead, behind


def residual_before(field, nu, turned, wrap, slopes, out):
    def one(step, _):
        f, t = step // 4, lax.rem(step, 4)
        rows = tile(t)
        mu = nu[f, tile(t + 1), :]
        for n in range(8):
            view = [field.at[f, n, c, pl.ds(pl.multiple_of(8 * t, 8), 24)] for c in range(3)]
            u0, u1 = view[0][8:16, :], view[1][8:16, :]
            for c in range(3):
                v, up, down = view[c][8:16, :], view[c][9:17, :], view[c][7:15, :]
                right, left = turned[0, f, n, c, rows, :], turned[1, f, n, c, rows, :]
                ahead, behind = times(turned, wrap, f, n, c, rows)
                along = 0.5 * (right - left)
                across = 0.5 * (up - down)
                slopes[f, n, 0, c, rows, :] = along
                slopes[f, n, 1, c, rows, :] = across
                lap = (right + left) + (up + down) - 6.0 * v
                pull = (ahead - behind) + (v - field[1 - f, n, c, tile(t + 1), :])
                out[f, n, c, rows, :] = 0.5 * pull + (u0 * along + u1 * across) - mu * lap
        return 0

    lax.fori_loop(0, 8, one, 0)


def residual_after(field, nu, turned, halo, force, partial, slopes, sides, out, cells, f):
    masks = residues()

    def one(t, _):
        rows, inner = tile(t), tile(t + 1)
        mu = nu[f, inner, :]
        for c in range(3):
            edges = Edges()
            high, low = halo[f, 0, c, rows, :], halo[f, 1, c, rows, :]
            for n in range(8):
                ahead = jnp.where(masks[(n + 7) % 8], high, turned[2, f, n, c, rows, :])
                behind = jnp.where(masks[n], low, turned[3, f, n, c, rows, :])
                slope = 0.5 * (ahead - behind)
                slopes[f, n, 2, c, rows, :] = slope
                if c == 2:
                    sides[0, f, n, rows, :] = ahead
                    sides[1, f, n, rows, :] = behind
                value = partial[f, n, c, rows, :] - force[f, n, c, rows, :]
                value = value + field[f, n, 2, inner, :] * slope - mu * (ahead + behind)
                out[f, n, c, inner, :] = value
                edges.add(masks, n, value)
            edges.store(cells, f, c, t)
        return 0

    lax.fori_loop(0, 4, one, 0)


def descent_before(field, res, nu, turned_u, turned, wrap, slopes, out):
    def one(step, _):
        f, t = step // 4, lax.rem(step, 4)
        rows, inner = tile(t), tile(t + 1)
        mus = nu.at[f, pl.ds(pl.multiple_of(8 * t, 8), 24)]
        mu, mu_up, mu_down = mus[8:16, :], mus[9:17, :], mus[7:15, :]
        for n in range(8):
            u1 = field.at[f, n, 1, pl.ds(pl.multiple_of(8 * t, 8), 24)]
            right0, left0 = 0.5 * turned_u[0, f, n, 0, rows, :], 0.5 * turned_u[1, f, n, 0, rows, :]
            up1, down1 = 0.5 * u1[9:17, :] + mu_up, 0.5 * u1[7:15, :] - mu_down
            centre = [res[f, n, e, inner, :] for e in range(3)]
            for c in range(3):
                r, view = centre[c], res.at[f, n, c, pl.ds(pl.multiple_of(8 * t, 8), 24)]
                right, left = turned[0, f, n, c, rows, :], turned[1, f, n, c, rows, :]
                ahead, behind = times(turned, wrap, f, n, c, rows)
                transport = centre[0] * slopes[f, n, c, 0, rows, :]
                transport = transport + centre[1] * slopes[f, n, c, 1, rows, :]
                transport = transport + centre[2] * slopes[f, n, c, 2, rows, :]
                flux = (right0 * right - left0 * left) + (up1 * view[9:17, :] - down1 * view[7:15, :])
                flux = flux + mu * ((right + left) - 6.0 * r)
                pull = (behind - ahead) + (r - res[1 - f, n, c, inner, :])
                descent = 0.5 * pull + (transport - flux)
                out[f, n, c, rows, :] = field[f, n, c, inner, :] - STEP * descent
        return 0

    lax.fori_loop(0, 8, one, 0)


def descent_after(nu, turned, halo, partial, sides, out, cells, f):
    masks = residues()

    def one(t, _):
        rows, inner = tile(t), tile(t + 1)
        mu = STEP * nu[f, inner, :]
        for c in range(3):
            edges = Edges()
            high, low = halo[f, 0, c, rows, :], halo[f, 1, c, rows, :]
            for n in range(8):
                ahead = jnp.where(masks[(n + 7) % 8], high, turned[2, f, n, c, rows, :])
                behind = jnp.where(masks[n], low, turned[3, f, n, c, rows, :])
                flux = sides[0, f, n, rows, :] * ahead - sides[1, f, n, rows, :] * behind
                value = partial[f, n, c, rows, :] + (0.5 * STEP * flux + mu * (ahead + behind))
                out[f, n, c, inner, :] = value
                if cells is not None:
                    edges.add(masks, n, value)
            if cells is not None:
                edges.store(cells, f, c, t)
        return 0

    lax.fori_loop(0, 4, one, 0)


def kernel(
    u_hbm, f_hbm, nu_in, out_r, out_u,
    raw_u, raw_f, pack_u, pack_f, field_a, field_b, force, res, partial, slopes, sides, nu,
    turned_u, turned_r, wrap, got_r, cells_out, cells_in, rows_out, rows_in, final,
    load_sem, self_sem, u_send, u_recv, f_send, f_recv, r_send, r_recv, o_send, o_recv,
    halo_send, halo_recv, nu_send, nu_recv,
):
    x, y, cls, z = position()
    xh = x // 2
    p = path_of(x, y)
    group = group_of(p, z)
    my_f, my_n = slot_of(x, y)
    rows = pl.ds(ROW0, 32)

    load_u = pltpu.make_async_copy(u_hbm, raw_u, load_sem.at[0])
    load_u.start()
    load_f = pltpu.make_async_copy(f_hbm, raw_f, load_sem.at[1])
    load_f.start()

    barrier = pltpu.get_barrier_semaphore()
    peers = [(lax.rem(x + dx, 4), lax.rem(y + dy, 4)) for dx, dy in OFFSETS]
    nx, ny, nz = along_path(p, z, 1)
    bx, by, bz = along_path(p, z, -1)
    ahead_dev, behind_dev = device_of(nx, ny, cls, nz), device_of(bx, by, cls, bz)
    other_core = device_of(x, y, 1 - cls, z)
    for px, py in peers:
        pl.semaphore_signal(barrier, inc=1, device_id=device_of(px, py, cls, z), device_id_type=MESH)
    for there in (
        other_core,
        device_of(x, y, cls, lax.rem(z + 1, 8)),
        device_of(x, y, cls, lax.rem(z + 7, 8)),
    ):
        pl.semaphore_signal(barrier, inc=1, device_id=there, device_id_type=MESH)

    row_id = lax.broadcasted_iota(jnp.int32, (8, 128), 0)
    for t in range(4):
        column = jnp.zeros((8, 128), jnp.float32)
        for s in range(8):
            r = 8 * t + s
            column = jnp.where(row_id == s, nu_in[r + xh * (31 - 2 * r)], column)
        nu[xh, ROW0 + 8 * t : ROW0 + 8 * t + 8, :] = column

    load_u.wait()
    pack(raw_u, pack_u, xh, my_n)
    pl.semaphore_wait(barrier, len(OFFSETS) + 3)

    def remote(src, dst, send, recv, there):
        return pltpu.make_async_remote_copy(
            src_ref=src, dst_ref=dst, send_sem=send, recv_sem=recv, device_id=there, device_id_type=MESH
        )

    pending = []
    u_in = []
    for j, (px, py) in enumerate(peers):
        copy = remote(
            pack_u.at[group_of(path_of(px, py), z)], field_a.at[my_f, my_n, :, rows],
            u_send.at[j], u_recv.at[j], device_of(px, py, cls, z),
        )
        copy.start()
        u_in.append(copy)
    own_u = pltpu.make_async_copy(pack_u.at[group], field_a.at[my_f, my_n, :, rows], self_sem.at[0])
    own_u.start()
    nu_copy = remote(nu.at[xh, rows], nu.at[xh, rows], nu_send, nu_recv, device_of(3 - x, y, cls, z))
    nu_copy.start()
    pending += u_in

    load_f.wait()
    pack(raw_f, pack_f, xh, my_n)
    f_in = []

    def send_force(c):
        for j, (px, py) in enumerate(peers):
            copy = remote(
                pack_f.at[group_of(path_of(px, py), z), c], force.at[my_f, my_n, c],
                f_send.at[c, j], f_recv.at[c, j], device_of(px, py, cls, z),
            )
            copy.start()
            f_in.append(copy)

    own_f = pltpu.make_async_copy(pack_f.at[group], force.at[my_f, my_n], self_sem.at[1])
    own_f.start()
    send_force(0)
    send_force(1)

    def send_cells(k, f):
        sends = [
            remote(
                cells_out.at[k, f, side], cells_in.at[k, f, side],
                halo_send.at[k, 2 * f + side], halo_recv.at[k, 2 * f + side], there,
            )
            for side, there in enumerate((behind_dev, ahead_dev))
        ]
        for copy in sends:
            copy.start()
        pending.extend(sends)
        return sends

    def send_rows(k, values):
        pack_rows(values, rows_out.at[k], final, cls)
        if k == 0:
            for f in range(2):
                edge = jnp.where(cls == 1, nu[f, ROW0 : ROW0 + 1, :], nu[f, ROW0 + 31 : ROW0 + 32, :])
                rows_out[k, f, 0, 3:4, :] = edge
        copy = remote(rows_out.at[k], rows_in.at[k], halo_send.at[k, 4], halo_recv.at[k, 4], other_core)
        copy.start()
        pending.append(copy)
        return copy

    def take_rows(k, values, copy):
        copy.wait_recv()
        fill_rows(values, rows_in.at[k], final, cls)
        if k == 0:
            for f in range(2):
                got = rows_in[k, f, 0, 3:4, :]
                fold = nu[1 - f, ROW0 + 31 : ROW0 + 32, :]
                nu[f, ROW0 - 1 : ROW0, :] = jnp.where(cls == 1, got, 0.0)
                nu[f, ROW0 + 32 : ROW0 + 33, :] = jnp.where(cls == 1, fold, got)

    def take_cells(sends):
        for copy in sends:
            copy.wait_recv()

    def residual_round(k, values, sends, last):
        edge = send_rows(k, values)
        rotate_all(values, turned_u, wrap)
        take_rows(k, values, edge)
        residual_before(values, nu, turned_u, wrap, slopes, partial)
        if not last:
            own_f.wait()
            for copy in f_in:
                copy.wait_recv()
        nexts = []
        for f in range(2):
            take_cells(sends[f])
            residual_after(
                values, nu, turned_u, cells_in.at[k], force, partial, slopes, sides, res,
                cells_out.at[k + 1], f,
            )
            nexts.append(send_cells(k + 1, f))
        return nexts

    def descent_round(k, values, sends, out, last):
        edge = send_rows(k, res)
        rotate_all(res, turned_r, wrap)
        take_rows(k, res, edge)
        descent_before(values, res, nu, turned_u, turned_r, wrap, slopes, partial)
        nexts = []
        for f in range(2):
            take_cells(sends[f])
            descent_after(
                nu, turned_r, cells_in.at[k], partial, sides, out,
                None if last else cells_out.at[k + 1], f,
            )
            if not last:
                nexts.append(send_cells(k + 1, f))
        return nexts

    def send_back(values, dst, send, recv):
        copies = []
        for j, (px, py) in enumerate(peers):
            f, n = slot_of(px, py)
            copy = remote(
                values.at[f, n, :, rows], dst.at[group], send.at[j], recv.at[j], device_of(px, py, cls, z)
            )
            copy.start()
            copies.append(copy)
        return copies

    nu_copy.wait()
    own_u.wait()
    take_cells(u_in)

    sends = []
    for f in range(2):
        pack_cells(field_a, cells_out.at[0], f)
        sends.append(send_cells(0, f))
    send_force(2)
    sends = residual_round(0, field_a, sends, False)
    pending += f_in
    sends = descent_round(1, field_a, sends, field_b, False)
    sends = residual_round(2, field_b, sends, True)

    r_out = send_back(res, got_r, r_send, r_recv)
    own_r = pltpu.make_async_copy(res.at[my_f, my_n, :, rows], got_r.at[group], self_sem.at[2])
    own_r.start()
    descent_round(3, field_b, sends, field_a, True)
    o_out = send_back(field_a, out_u, o_send, o_recv)
    own_o = pltpu.make_async_copy(field_a.at[my_f, my_n, :, rows], out_u.at[group], self_sem.at[3])
    own_o.start()

    own_r.wait()
    take_cells(r_out)
    unpack(got_r, raw_u, xh, my_n)
    store_r = pltpu.make_async_copy(raw_u, out_r, load_sem.at[0])
    store_r.start()
    for copy in pending + r_out:
        copy.wait_send()
    store_r.wait()
    own_o.wait()
    for copy in o_out:
        copy.wait()


def finish(u_hbm, r_hbm, u_out, r_out, packed, plain, passed, u_load, u_store, r_sem):
    x, y, _, _ = position()
    xh = x // 2
    _, n = slot_of(x, y)
    loads, stores = [], []
    for t in range(4):
        here, there = tile(t), tile(t + xh * (3 - 2 * t))
        loads.append(pltpu.make_async_copy(u_hbm.at[:, :, there], packed.at[:, :, there], u_load.at[t]))
        stores.append(pltpu.make_async_copy(plain.at[:, :, here], u_out.at[:, :, here], u_store.at[t]))
        loads[-1].start()
    through = pltpu.make_async_copy(r_hbm, passed, r_sem.at[0])
    through.start()
    for t in range(4):
        loads[t].wait()
        unpack_rows(packed, plain, xh, n, t)
        stores[t].start()
        if t == 0:
            through.wait()
            onward = pltpu.make_async_copy(passed, r_out, r_sem.at[1])
            onward.start()
    for copy in stores + [onward]:
        copy.wait()


def local(starting_speed_vector, driving_source, viscosity):
    block = starting_speed_vector.shape
    f32 = jnp.float32
    flat = (3, 16, 32, 128)
    plain, packed = pltpu.VMEM(flat, f32), pltpu.VMEM((16, 3, 32, 128), f32)
    slabs, padded = pltpu.VMEM((2, 8, 3, 32, 128), f32), pltpu.VMEM((2, 8, 3, 48, 128), f32)
    turned = pltpu.VMEM((4, 2, 8, 3, 32, 128), f32)
    cells = pltpu.VMEM((4, 2, 2, 3, 32, 128), f32)
    edge = pltpu.VMEM((4, 2, 8, 8, 128), f32)
    dma = pltpu.SemaphoreType.DMA
    anywhere = pl.BlockSpec(memory_space=pl.ANY)
    got_r, got_u = pl.pallas_call(
        kernel,
        out_shape=(jax.ShapeDtypeStruct(flat, f32), jax.ShapeDtypeStruct((16, 3, 32, 128), f32)),
        in_specs=[anywhere, anywhere, pl.BlockSpec(memory_space=pltpu.SMEM)],
        out_specs=(anywhere, anywhere),
        scratch_shapes=[
            plain, plain, packed, packed, padded, padded, slabs, padded, slabs,
            pltpu.VMEM((2, 8, 3, 3, 32, 128), f32),
            pltpu.VMEM((2, 2, 8, 32, 128), f32),
            pltpu.VMEM((2, 48, 128), f32),
            turned, turned,
            pltpu.VMEM((2, 2, 3, 32, 128), f32),
            packed, cells, cells, edge, edge,
            pltpu.VMEM((2, 8, 8, 128), f32),
            dma((2,)), dma((4,)),
            dma((15,)), dma((15,)), dma((3, 15)), dma((3, 15)),
            dma((15,)), dma((15,)), dma((15,)), dma((15,)),
            dma((4, 5)), dma((4, 5)), dma(()), dma(()),
        ],
        compiler_params=pltpu.CompilerParams(collective_id=0, has_side_effects=True),
        name="descend",
    )(starting_speed_vector.reshape(flat), driving_source.reshape(flat), viscosity)
    orbit, residual = pl.pallas_call(
        finish,
        out_shape=(jax.ShapeDtypeStruct(flat, f32), jax.ShapeDtypeStruct(flat, f32)),
        in_specs=[anywhere, anywhere],
        out_specs=(anywhere, anywhere),
        scratch_shapes=[packed, plain, plain, dma((4,)), dma((4,)), dma((2,))],
        name="finish",
    )(got_u, got_r)
    return orbit.reshape(block), residual.reshape(block)


def solution(mesh):
    spec = P(None, "tm", None, "wall", "span")
    return jax.shard_map(
        local, mesh=mesh, in_specs=(spec, spec, P("wall")), out_specs=(spec, spec), check_vma=False
    )
```

```python
import jax
import jax.numpy as jnp
from jax import lax
from jax.experimental import pallas as pl
from jax.experimental.pallas import tpu as pltpu
from jax.sharding import PartitionSpec as P

STEP = 0.05
SIGN = (1.0, -1.0, 1.0)
MESH = pl.DeviceIdType.MESH
OFFSETS = sorted(
    ((dx, dy) for dx in range(4) for dy in range(4) if (dx, dy) != (0, 0)),
    key=lambda o: -(min(o[0], 4 - o[0]) + min(o[1], 4 - o[1])),
)
ROW0 = 8


def roll(v, shift, axis=1):
    return pltpu.roll(v, shift % 128 if isinstance(shift, int) else shift, axis)


def device_of(x, y, cls, z):
    xh, xl = x // 2, lax.rem(x, 2)
    return (xl * 4 + y, xh * 2 + (cls + xh - 2 * cls * xh), z)


def position():
    tm, wall, z = lax.axis_index("tm"), lax.axis_index("wall"), lax.axis_index("span")
    xl, y, xh, core = tm // 4, lax.rem(tm, 4), wall // 2, lax.rem(wall, 2)
    return xh * 2 + xl, y, core + xh - 2 * core * xh, z


def path_of(x, y):
    odd = lax.rem(y, 2)
    return 4 * y + x + odd * (3 - 2 * x)


def chip_at(p):
    y, a = p // 4, lax.rem(p, 4)
    odd = lax.rem(y, 2)
    return a + odd * (3 - 2 * a), y


def group_of(p, z):
    return p + lax.rem(z, 2) * (15 - 2 * p)


def slot_of(x, y):
    xh, xl = x // 2, lax.rem(x, 2)
    return xh, lax.rem(4 * xl + y + 4 * xh, 8)


def along_path(p, z, way):
    there = p + way * (1 - 2 * lax.rem(z, 2))
    over = (there + 16) // 16 - 1
    over = over * over
    x, y = chip_at(there * (1 - over) + p * over)
    return x, y, lax.rem(z + way * over + 8, 8)


def swap_groups(ins, before=0, after=0):
    lane = lax.broadcasted_iota(jnp.int32, (8, 128), 1)
    turned = [roll(v, lax.rem(8 * i + before + 128, 128)) for i, v in enumerate(ins)]
    mixed = [turned[-d % 16] for d in range(16)]
    for bit in range(4):
        mask = (lane & (8 << bit)) != 0
        mixed = [jnp.where(mask, mixed[(d - (1 << bit)) % 16], mixed[d]) for d in range(16)]
    return [roll(v, lax.rem(128 - 8 * d + after, 128)) for d, v in enumerate(mixed)]


def frame_rows(v, xh):
    row = lax.broadcasted_iota(jnp.int32, (8, 128), 0)
    return jnp.take_along_axis(v, row + xh * (7 - 2 * row), axis=0, mode="promise_in_bounds")


def frame_sign(v, c, xh):
    return v * (1.0 - 2.0 * xh.astype(jnp.float32)) if SIGN[c] < 0 else v


def tile(t):
    return pl.ds(pl.multiple_of(8 * t, 8), 8)


def pack(src, dst, xh, n):
    def one(t, _):
        to = tile(t + xh * (3 - 2 * t))
        for c in range(3):
            ins = [src[c, i, tile(t), :] for i in range(16)]
            for d, v in enumerate(swap_groups(ins, 0, n)):
                dst[d, c, to, :] = frame_sign(frame_rows(v, xh), c, xh)
        return 0

    lax.fori_loop(0, 4, one, 0)


def unpack_rows(src, dst, xh, n, t):
    to = tile(t + xh * (3 - 2 * t))
    for c in range(3):
        ins = [src[d, c, to, :] for d in range(16)]
        for i, v in enumerate(swap_groups(ins, -n, 0)):
            dst[c, i, tile(t), :] = frame_sign(frame_rows(v, xh), c, xh)


def unpack(src, dst, xh, n):
    def one(t, _):
        unpack_rows(src, dst, xh, n, t)
        return 0

    lax.fori_loop(0, 4, one, 0)


def residues():
    lane = lax.broadcasted_iota(jnp.int32, (8, 128), 1) & 7
    return [lane == q for q in range(8)]


class Edges:
    def __init__(self):
        self.first = self.last = None

    def add(self, masks, n, v):
        self.first = v if n == 0 else jnp.where(masks[n], v, self.first)
        self.last = v if n == 0 else jnp.where(masks[(n + 7) % 8], v, self.last)

    def store(self, out, f, c, t):
        out[0, f, c, tile(t), :] = roll(self.first, 7)
        out[1, f, c, tile(t), :] = roll(self.last, -7)


def pack_cells(field, out, h):
    masks = residues()

    def one(step, _):
        f, part = step // 2, lax.rem(step, 2)
        for c in range(3):
            edges = Edges()
            for n in range(8):
                edges.add(masks, n, field[f, n, c, tile(part + 2 * h + 1), :])
            edges.store(out, f, c, part)
        return 0

    lax.fori_loop(0, 4, one, 0)


def pack_rows(field, edge, final, cls):
    for f in range(2):
        for n in range(8):
            for c in range(3):
                first = field[f, n, c, ROW0 : ROW0 + 1, :]
                last = field[f, n, c, ROW0 + 31 : ROW0 + 32, :]
                edge[f, n, c : c + 1, :] = jnp.where(cls == 1, first, last)
                final[f, n, c : c + 1, :] = last


def fill_rows(field, edge, final, cls):
    row = lax.broadcasted_iota(jnp.int32, (8, 128), 0)
    sign = jnp.where(row == 1, SIGN[1], 1.0)
    for f in range(2):
        for n in range(8):
            got = edge[f, n]
            fold = sign * roll(final[1 - f, (n + 4) % 8], -4 if n < 4 else 4)
            low = jnp.where(cls == 1, got, 0.0)
            high = jnp.where(cls == 1, fold, got)
            for c in range(3):
                field[f, n, c, ROW0 - 1 : ROW0, :] = low[c : c + 1, :]
                field[f, n, c, ROW0 + 32 : ROW0 + 33, :] = high[c : c + 1, :]


def rotate_all(field, turned, wrap):
    def one(f, _):
        for c in range(3):
            for t in range(4):
                rows, out = slice(ROW0 + 8 * t, ROW0 + 8 * t + 8), slice(8 * t, 8 * t + 8)
                for n in range(8):
                    v = field[f, n, c, rows, :]
                    for kind, shift in enumerate((-8, 8, -1, 1)):
                        turned[kind, f, n, c, out, :] = roll(v, shift)
                    if n == 0:
                        wrap[0, f, c, out, :] = roll(v, 7)
                    if n == 7:
                        wrap[1, f, c, out, :] = roll(v, -7)
        return 0

    lax.fori_loop(0, 2, one, 0)


def times(turned, wrap, f, n, c, rows):
    ahead = wrap[0, f, c, rows, :] if n == 7 else turned[2, f, n + 1, c, rows, :]
    behind = wrap[1, f, c, rows, :] if n == 0 else turned[3, f, n - 1, c, rows, :]
    return ahead, behind


def residual_before(field, nu, turned, wrap, slopes, out):
    def one(step, _):
        f, t = step // 4, lax.rem(step, 4)
        rows = tile(t)
        mu = nu[f, tile(t + 1), :]
        for n in range(8):
            view = [field.at[f, n, c, pl.ds(pl.multiple_of(8 * t, 8), 24)] for c in range(3)]
            u0, u1 = view[0][8:16, :], view[1][8:16, :]
            for c in range(3):
                v, up, down = view[c][8:16, :], view[c][9:17, :], view[c][7:15, :]
                right, left = turned[0, f, n, c, rows, :], turned[1, f, n, c, rows, :]
                ahead, behind = times(turned, wrap, f, n, c, rows)
                along = 0.5 * (right - left)
                across = 0.5 * (up - down)
                slopes[f, n, 0, c, rows, :] = along
                slopes[f, n, 1, c, rows, :] = across
                lap = (right + left) + (up + down) - 6.0 * v
                pull = (ahead - behind) + (v - field[1 - f, n, c, tile(t + 1), :])
                out[f, n, c, rows, :] = 0.5 * pull + (u0 * along + u1 * across) - mu * lap
        return 0

    lax.fori_loop(0, 8, one, 0)


def residual_after(field, nu, turned, halo, force, partial, slopes, sides, out, cells, h):
    masks = residues()

    def one(step, _):
        f, part = step // 2, lax.rem(step, 2)
        t = part + 2 * h
        rows, inner = tile(t), tile(t + 1)
        mu = nu[f, inner, :]
        for c in range(3):
            edges = Edges()
            high, low = halo[0, f, c, tile(part), :], halo[1, f, c, tile(part), :]
            for n in range(8):
                ahead = jnp.where(masks[(n + 7) % 8], high, turned[2, f, n, c, rows, :])
                behind = jnp.where(masks[n], low, turned[3, f, n, c, rows, :])
                slope = 0.5 * (ahead - behind)
                slopes[f, n, 2, c, rows, :] = slope
                if c == 2:
                    sides[0, f, n, rows, :] = ahead
                    sides[1, f, n, rows, :] = behind
                value = partial[f, n, c, rows, :] - force[f, n, c, rows, :]
                value = value + field[f, n, 2, inner, :] * slope - mu * (ahead + behind)
                out[f, n, c, inner, :] = value
                edges.add(masks, n, value)
            edges.store(cells, f, c, part)
        return 0

    lax.fori_loop(0, 4, one, 0)


def descent_before(field, res, nu, turned_u, turned, wrap, slopes, out):
    def one(step, _):
        f, t = step // 4, lax.rem(step, 4)
        rows, inner = tile(t), tile(t + 1)
        mus = nu.at[f, pl.ds(pl.multiple_of(8 * t, 8), 24)]
        mu, mu_up, mu_down = mus[8:16, :], mus[9:17, :], mus[7:15, :]
        for n in range(8):
            u1 = field.at[f, n, 1, pl.ds(pl.multiple_of(8 * t, 8), 24)]
            right0, left0 = 0.5 * turned_u[0, f, n, 0, rows, :], 0.5 * turned_u[1, f, n, 0, rows, :]
            up1, down1 = 0.5 * u1[9:17, :] + mu_up, 0.5 * u1[7:15, :] - mu_down
            centre = [res[f, n, e, inner, :] for e in range(3)]
            for c in range(3):
                r, view = centre[c], res.at[f, n, c, pl.ds(pl.multiple_of(8 * t, 8), 24)]
                right, left = turned[0, f, n, c, rows, :], turned[1, f, n, c, rows, :]
                ahead, behind = times(turned, wrap, f, n, c, rows)
                transport = centre[0] * slopes[f, n, c, 0, rows, :]
                transport = transport + centre[1] * slopes[f, n, c, 1, rows, :]
                transport = transport + centre[2] * slopes[f, n, c, 2, rows, :]
                flux = (right0 * right - left0 * left) + (up1 * view[9:17, :] - down1 * view[7:15, :])
                flux = flux + mu * ((right + left) - 6.0 * r)
                pull = (behind - ahead) + (r - res[1 - f, n, c, inner, :])
                descent = 0.5 * pull + (transport - flux)
                out[f, n, c, rows, :] = field[f, n, c, inner, :] - STEP * descent
        return 0

    lax.fori_loop(0, 8, one, 0)


def descent_after(nu, turned, halo, partial, sides, out, cells, h):
    masks = residues()

    def one(step, _):
        f, part = step // 2, lax.rem(step, 2)
        t = part + 2 * h
        rows, inner = tile(t), tile(t + 1)
        mu = STEP * nu[f, inner, :]
        for c in range(3):
            edges = Edges()
            high, low = halo[0, f, c, tile(part), :], halo[1, f, c, tile(part), :]
            for n in range(8):
                ahead = jnp.where(masks[(n + 7) % 8], high, turned[2, f, n, c, rows, :])
                behind = jnp.where(masks[n], low, turned[3, f, n, c, rows, :])
                flux = sides[0, f, n, rows, :] * ahead - sides[1, f, n, rows, :] * behind
                value = partial[f, n, c, rows, :] + (0.5 * STEP * flux + mu * (ahead + behind))
                out[f, n, c, inner, :] = value
                if cells is not None:
                    edges.add(masks, n, value)
            if cells is not None:
                edges.store(cells, f, c, part)
        return 0

    lax.fori_loop(0, 4, one, 0)


def kernel(
    u_hbm, f_hbm, nu_in, out_r, out_u,
    raw_u, raw_f, pack_u, pack_f, field_a, field_b, force, res, partial, slopes, sides, nu,
    turned_u, turned_r, wrap, got_r, cells_out, cells_in, rows_out, rows_in, final,
    load_sem, self_sem, u_send, u_recv, f_send, f_recv, r_send, r_recv, o_send, o_recv,
    halo_send, halo_recv, nu_send, nu_recv,
):
    x, y, cls, z = position()
    xh = x // 2
    p = path_of(x, y)
    group = group_of(p, z)
    my_f, my_n = slot_of(x, y)
    rows = pl.ds(ROW0, 32)

    load_u = pltpu.make_async_copy(u_hbm, raw_u, load_sem.at[0])
    load_u.start()
    load_f = pltpu.make_async_copy(f_hbm, raw_f, load_sem.at[1])
    load_f.start()

    barrier = pltpu.get_barrier_semaphore()
    peers = [(lax.rem(x + dx, 4), lax.rem(y + dy, 4)) for dx, dy in OFFSETS]
    nx, ny, nz = along_path(p, z, 1)
    bx, by, bz = along_path(p, z, -1)
    ahead_dev, behind_dev = device_of(nx, ny, cls, nz), device_of(bx, by, cls, bz)
    other_core = device_of(x, y, 1 - cls, z)
    for px, py in peers:
        pl.semaphore_signal(barrier, inc=1, device_id=device_of(px, py, cls, z), device_id_type=MESH)
    for there in (
        other_core,
        device_of(x, y, cls, lax.rem(z + 1, 8)),
        device_of(x, y, cls, lax.rem(z + 7, 8)),
    ):
        pl.semaphore_signal(barrier, inc=1, device_id=there, device_id_type=MESH)

    row_id = lax.broadcasted_iota(jnp.int32, (8, 128), 0)
    for t in range(4):
        column = jnp.zeros((8, 128), jnp.float32)
        for s in range(8):
            r = 8 * t + s
            column = jnp.where(row_id == s, nu_in[r + xh * (31 - 2 * r)], column)
        nu[xh, ROW0 + 8 * t : ROW0 + 8 * t + 8, :] = column

    load_u.wait()
    pack(raw_u, pack_u, xh, my_n)
    pl.semaphore_wait(barrier, len(OFFSETS) + 3)

    def remote(src, dst, send, recv, there):
        return pltpu.make_async_remote_copy(
            src_ref=src, dst_ref=dst, send_sem=send, recv_sem=recv, device_id=there, device_id_type=MESH
        )

    pending = []
    u_in = []
    for j, (px, py) in enumerate(peers):
        copy = remote(
            pack_u.at[group_of(path_of(px, py), z)], field_a.at[my_f, my_n, :, rows],
            u_send.at[j], u_recv.at[j], device_of(px, py, cls, z),
        )
        copy.start()
        u_in.append(copy)
    own_u = pltpu.make_async_copy(pack_u.at[group], field_a.at[my_f, my_n, :, rows], self_sem.at[0])
    own_u.start()
    nu_copy = remote(nu.at[xh, rows], nu.at[xh, rows], nu_send, nu_recv, device_of(3 - x, y, cls, z))
    nu_copy.start()
    pending += u_in

    load_f.wait()
    pack(raw_f, pack_f, xh, my_n)
    f_in = []

    def send_force(h):
        half = pl.ds(16 * h, 16)
        for j, (px, py) in enumerate(peers):
            copy = remote(
                pack_f.at[group_of(path_of(px, py), z), :, half], force.at[my_f, my_n, :, half],
                f_send.at[h, j], f_recv.at[h, j], device_of(px, py, cls, z),
            )
            copy.start()
            f_in.append(copy)

    own_f = pltpu.make_async_copy(pack_f.at[group], force.at[my_f, my_n], self_sem.at[1])
    own_f.start()
    send_force(0)

    def send_cells(k, h):
        sends = [
            remote(
                cells_out.at[k, h, side], cells_in.at[k, h, side],
                halo_send.at[k, 2 * h + side], halo_recv.at[k, 2 * h + side], there,
            )
            for side, there in enumerate((behind_dev, ahead_dev))
        ]
        for copy in sends:
            copy.start()
        pending.extend(sends)
        return sends

    def send_rows(k, values):
        pack_rows(values, rows_out.at[k], final, cls)
        if k == 0:
            for f in range(2):
                edge = jnp.where(cls == 1, nu[f, ROW0 : ROW0 + 1, :], nu[f, ROW0 + 31 : ROW0 + 32, :])
                rows_out[k, f, 0, 3:4, :] = edge
        copy = remote(rows_out.at[k], rows_in.at[k], halo_send.at[k, 4], halo_recv.at[k, 4], other_core)
        copy.start()
        pending.append(copy)
        return copy

    def take_rows(k, values, copy):
        copy.wait_recv()
        fill_rows(values, rows_in.at[k], final, cls)
        if k == 0:
            for f in range(2):
                got = rows_in[k, f, 0, 3:4, :]
                fold = nu[1 - f, ROW0 + 31 : ROW0 + 32, :]
                nu[f, ROW0 - 1 : ROW0, :] = jnp.where(cls == 1, got, 0.0)
                nu[f, ROW0 + 32 : ROW0 + 33, :] = jnp.where(cls == 1, fold, got)

    def take_cells(sends):
        for copy in sends:
            copy.wait_recv()

    def residual_round(k, values, sends, last):
        edge = send_rows(k, values)
        rotate_all(values, turned_u, wrap)
        take_rows(k, values, edge)
        residual_before(values, nu, turned_u, wrap, slopes, partial)
        if not last:
            own_f.wait()
        nexts = []
        for h in range(2):
            take_cells(sends[h])
            if not last:
                take_cells(f_in[15 * h : 15 * h + 15])
            residual_after(
                values, nu, turned_u, cells_in.at[k, h], force, partial, slopes, sides, res,
                cells_out.at[k + 1, h], h,
            )
            nexts.append(send_cells(k + 1, h))
        return nexts

    def descent_round(k, values, sends, out, last):
        edge = send_rows(k, res)
        rotate_all(res, turned_r, wrap)
        take_rows(k, res, edge)
        descent_before(values, res, nu, turned_u, turned_r, wrap, slopes, partial)
        nexts = []
        for h in range(2):
            take_cells(sends[h])
            descent_after(
                nu, turned_r, cells_in.at[k, h], partial, sides, out,
                None if last else cells_out.at[k + 1, h], h,
            )
            if not last:
                nexts.append(send_cells(k + 1, h))
        return nexts

    def send_back(values, dst, send, recv):
        copies = []
        for j, (px, py) in enumerate(peers):
            f, n = slot_of(px, py)
            copy = remote(
                values.at[f, n, :, rows], dst.at[group], send.at[j], recv.at[j], device_of(px, py, cls, z)
            )
            copy.start()
            copies.append(copy)
        return copies

    nu_copy.wait()
    own_u.wait()
    take_cells(u_in)

    sends = []
    for h in range(2):
        pack_cells(field_a, cells_out.at[0, h], h)
        sends.append(send_cells(0, h))
    send_force(1)
    sends = residual_round(0, field_a, sends, False)
    pending += f_in
    sends = descent_round(1, field_a, sends, field_b, False)
    sends = residual_round(2, field_b, sends, True)

    r_out = send_back(res, got_r, r_send, r_recv)
    own_r = pltpu.make_async_copy(res.at[my_f, my_n, :, rows], got_r.at[group], self_sem.at[2])
    own_r.start()
    descent_round(3, field_b, sends, field_a, True)
    o_out = send_back(field_a, out_u, o_send, o_recv)
    own_o = pltpu.make_async_copy(field_a.at[my_f, my_n, :, rows], out_u.at[group], self_sem.at[3])
    own_o.start()

    own_r.wait()
    take_cells(r_out)
    unpack(got_r, raw_u, xh, my_n)
    store_r = pltpu.make_async_copy(raw_u, out_r, load_sem.at[0])
    store_r.start()
    for copy in pending + r_out:
        copy.wait_send()
    store_r.wait()
    own_o.wait()
    for copy in o_out:
        copy.wait()


def finish(u_hbm, r_hbm, u_out, r_out, packed, plain, passed, u_load, u_store, r_sem):
    x, y, _, _ = position()
    xh = x // 2
    _, n = slot_of(x, y)
    loads, stores = [], []
    for t in range(4):
        here, there = tile(t), tile(t + xh * (3 - 2 * t))
        loads.append(pltpu.make_async_copy(u_hbm.at[:, :, there], packed.at[:, :, there], u_load.at[t]))
        stores.append(pltpu.make_async_copy(plain.at[:, :, here], u_out.at[:, :, here], u_store.at[t]))
        loads[-1].start()
    through = pltpu.make_async_copy(r_hbm, passed, r_sem.at[0])
    through.start()
    for t in range(4):
        loads[t].wait()
        unpack_rows(packed, plain, xh, n, t)
        stores[t].start()
        if t == 0:
            through.wait()
            onward = pltpu.make_async_copy(passed, r_out, r_sem.at[1])
            onward.start()
    for copy in stores + [onward]:
        copy.wait()


def local(starting_speed_vector, driving_source, viscosity):
    block = starting_speed_vector.shape
    f32 = jnp.float32
    flat = (3, 16, 32, 128)
    plain, packed = pltpu.VMEM(flat, f32), pltpu.VMEM((16, 3, 32, 128), f32)
    slabs, padded = pltpu.VMEM((2, 8, 3, 32, 128), f32), pltpu.VMEM((2, 8, 3, 48, 128), f32)
    turned = pltpu.VMEM((4, 2, 8, 3, 32, 128), f32)
    cells = pltpu.VMEM((4, 2, 2, 2, 3, 16, 128), f32)
    edge = pltpu.VMEM((4, 2, 8, 8, 128), f32)
    dma = pltpu.SemaphoreType.DMA
    anywhere = pl.BlockSpec(memory_space=pl.ANY)
    got_r, got_u = pl.pallas_call(
        kernel,
        out_shape=(jax.ShapeDtypeStruct(flat, f32), jax.ShapeDtypeStruct((16, 3, 32, 128), f32)),
        in_specs=[anywhere, anywhere, pl.BlockSpec(memory_space=pltpu.SMEM)],
        out_specs=(anywhere, anywhere),
        scratch_shapes=[
            plain, plain, packed, packed, padded, padded, slabs, padded, slabs,
            pltpu.VMEM((2, 8, 3, 3, 32, 128), f32),
            pltpu.VMEM((2, 2, 8, 32, 128), f32),
            pltpu.VMEM((2, 48, 128), f32),
            turned, turned,
            pltpu.VMEM((2, 2, 3, 32, 128), f32),
            packed, cells, cells, edge, edge,
            pltpu.VMEM((2, 8, 8, 128), f32),
            dma((2,)), dma((4,)),
            dma((15,)), dma((15,)), dma((2, 15)), dma((2, 15)),
            dma((15,)), dma((15,)), dma((15,)), dma((15,)),
            dma((4, 5)), dma((4, 5)), dma(()), dma(()),
        ],
        compiler_params=pltpu.CompilerParams(collective_id=0, has_side_effects=True),
        name="descend",
    )(starting_speed_vector.reshape(flat), driving_source.reshape(flat), viscosity)
    orbit, residual = pl.pallas_call(
        finish,
        out_shape=(jax.ShapeDtypeStruct(flat, f32), jax.ShapeDtypeStruct(flat, f32)),
        in_specs=[anywhere, anywhere],
        out_specs=(anywhere, anywhere),
        scratch_shapes=[packed, plain, plain, dma((4,)), dma((4,)), dma((2,))],
        name="finish",
    )(got_u, got_r)
    return orbit.reshape(block), residual.reshape(block)


def solution(mesh):
    spec = P(None, "tm", None, "wall", "span")
    return jax.shard_map(
        local, mesh=mesh, in_specs=(spec, spec, P("wall")), out_specs=(spec, spec), check_vma=False
    )
```

```python
import jax
import jax.numpy as jnp
from jax import lax
from jax.experimental import pallas as pl
from jax.experimental.pallas import tpu as pltpu
from jax.sharding import PartitionSpec as P

STEP = 0.05
SIGN = (1.0, -1.0, 1.0)
MESH = pl.DeviceIdType.MESH
OFFSETS = sorted(
    ((dx, dy) for dx in range(4) for dy in range(4) if (dx, dy) != (0, 0)),
    key=lambda o: -(min(o[0], 4 - o[0]) + min(o[1], 4 - o[1])),
)
ROW0 = 8


def roll(v, shift, axis=1):
    return pltpu.roll(v, shift % 128 if isinstance(shift, int) else shift, axis)


def device_of(x, y, cls, z):
    xh, xl = x // 2, lax.rem(x, 2)
    return (xl * 4 + y, xh * 2 + (cls + xh - 2 * cls * xh), z)


def position():
    tm, wall, z = lax.axis_index("tm"), lax.axis_index("wall"), lax.axis_index("span")
    xl, y, xh, core = tm // 4, lax.rem(tm, 4), wall // 2, lax.rem(wall, 2)
    return xh * 2 + xl, y, core + xh - 2 * core * xh, z


def path_of(x, y):
    odd = lax.rem(y, 2)
    return 4 * y + x + odd * (3 - 2 * x)


def chip_at(p):
    y, a = p // 4, lax.rem(p, 4)
    odd = lax.rem(y, 2)
    return a + odd * (3 - 2 * a), y


def group_of(p, z):
    return p + lax.rem(z, 2) * (15 - 2 * p)


def slot_of(x, y):
    xh, xl = x // 2, lax.rem(x, 2)
    return xh, lax.rem(4 * xl + y + 4 * xh, 8)


def along_path(p, z, way):
    there = p + way * (1 - 2 * lax.rem(z, 2))
    over = (there + 16) // 16 - 1
    over = over * over
    x, y = chip_at(there * (1 - over) + p * over)
    return x, y, lax.rem(z + way * over + 8, 8)


def swap_groups(ins, before=0, after=0):
    lane = lax.broadcasted_iota(jnp.int32, (8, 128), 1)
    turned = [roll(v, lax.rem(8 * i + before + 128, 128)) for i, v in enumerate(ins)]
    mixed = [turned[-d % 16] for d in range(16)]
    for bit in range(4):
        mask = (lane & (8 << bit)) != 0
        mixed = [jnp.where(mask, mixed[(d - (1 << bit)) % 16], mixed[d]) for d in range(16)]
    return [roll(v, lax.rem(128 - 8 * d + after, 128)) for d, v in enumerate(mixed)]


def frame_rows(v, xh):
    row = lax.broadcasted_iota(jnp.int32, (8, 128), 0)
    return jnp.take_along_axis(v, row + xh * (7 - 2 * row), axis=0, mode="promise_in_bounds")


def frame_sign(v, c, xh):
    return v * (1.0 - 2.0 * xh.astype(jnp.float32)) if SIGN[c] < 0 else v


def tile(t):
    return pl.ds(pl.multiple_of(8 * t, 8), 8)


def pack(src, dst, xh, n):
    def one(t, _):
        to = tile(t + xh * (3 - 2 * t))
        for c in range(3):
            ins = [src[c, i, tile(t), :] for i in range(16)]
            for d, v in enumerate(swap_groups(ins, 0, n)):
                dst[d, c, to, :] = frame_sign(frame_rows(v, xh), c, xh)
        return 0

    lax.fori_loop(0, 4, one, 0)


def unpack_rows(src, dst, xh, n, t):
    to = tile(t + xh * (3 - 2 * t))
    for c in range(3):
        ins = [src[d, c, to, :] for d in range(16)]
        for i, v in enumerate(swap_groups(ins, -n, 0)):
            dst[c, i, tile(t), :] = frame_sign(frame_rows(v, xh), c, xh)


def unpack(src, dst, xh, n):
    def one(t, _):
        unpack_rows(src, dst, xh, n, t)
        return 0

    lax.fori_loop(0, 4, one, 0)


def residues():
    lane = lax.broadcasted_iota(jnp.int32, (8, 128), 1) & 7
    return [lane == q for q in range(8)]


class Edges:
    def __init__(self):
        self.first = self.last = None

    def add(self, masks, n, v):
        self.first = v if n == 0 else jnp.where(masks[n], v, self.first)
        self.last = v if n == 0 else jnp.where(masks[(n + 7) % 8], v, self.last)

    def store(self, out, f, c):
        out[0, f, c] = roll(self.first, 7)
        out[1, f, c] = roll(self.last, -7)


def pack_cells(field, out, t):
    masks = residues()

    def one(f, _):
        for c in range(3):
            edges = Edges()
            for n in range(8):
                edges.add(masks, n, field[f, n, c, ROW0 + 8 * t : ROW0 + 8 * t + 8, :])
            edges.store(out, f, c)
        return 0

    lax.fori_loop(0, 2, one, 0)


def pack_rows(field, edge, final, cls):
    for f in range(2):
        for n in range(8):
            for c in range(3):
                first = field[f, n, c, ROW0 : ROW0 + 1, :]
                last = field[f, n, c, ROW0 + 31 : ROW0 + 32, :]
                edge[f, n, c : c + 1, :] = jnp.where(cls == 1, first, last)
                final[f, n, c : c + 1, :] = last


def fill_rows(field, edge, final, cls):
    row = lax.broadcasted_iota(jnp.int32, (8, 128), 0)
    sign = jnp.where(row == 1, SIGN[1], 1.0)
    for f in range(2):
        for n in range(8):
            got = edge[f, n]
            fold = sign * roll(final[1 - f, (n + 4) % 8], -4 if n < 4 else 4)
            low = jnp.where(cls == 1, got, 0.0)
            high = jnp.where(cls == 1, fold, got)
            for c in range(3):
                field[f, n, c, ROW0 - 1 : ROW0, :] = low[c : c + 1, :]
                field[f, n, c, ROW0 + 32 : ROW0 + 33, :] = high[c : c + 1, :]


def rotate_all(field, turned, wrap):
    def one(f, _):
        for c in range(3):
            for t in range(4):
                rows, out = slice(ROW0 + 8 * t, ROW0 + 8 * t + 8), slice(8 * t, 8 * t + 8)
                for n in range(8):
                    v = field[f, n, c, rows, :]
                    for kind, shift in enumerate((-8, 8, -1, 1)):
                        turned[kind, f, n, c, out, :] = roll(v, shift)
                    if n == 0:
                        wrap[0, f, c, out, :] = roll(v, 7)
                    if n == 7:
                        wrap[1, f, c, out, :] = roll(v, -7)
        return 0

    lax.fori_loop(0, 2, one, 0)


def times(turned, wrap, f, n, c, rows):
    ahead = wrap[0, f, c, rows, :] if n == 7 else turned[2, f, n + 1, c, rows, :]
    behind = wrap[1, f, c, rows, :] if n == 0 else turned[3, f, n - 1, c, rows, :]
    return ahead, behind


def residual_before(field, nu, turned, wrap, slopes, out):
    def one(step, _):
        f, t = step // 4, lax.rem(step, 4)
        rows = tile(t)
        mu = nu[f, tile(t + 1), :]
        for n in range(8):
            view = [field.at[f, n, c, pl.ds(pl.multiple_of(8 * t, 8), 24)] for c in range(3)]
            u0, u1 = view[0][8:16, :], view[1][8:16, :]
            for c in range(3):
                v, up, down = view[c][8:16, :], view[c][9:17, :], view[c][7:15, :]
                right, left = turned[0, f, n, c, rows, :], turned[1, f, n, c, rows, :]
                ahead, behind = times(turned, wrap, f, n, c, rows)
                along = 0.5 * (right - left)
                across = 0.5 * (up - down)
                slopes[f, n, 0, c, rows, :] = along
                slopes[f, n, 1, c, rows, :] = across
                lap = (right + left) + (up + down) - 6.0 * v
                pull = (ahead - behind) + (v - field[1 - f, n, c, tile(t + 1), :])
                out[f, n, c, rows, :] = 0.5 * pull + (u0 * along + u1 * across) - mu * lap
        return 0

    lax.fori_loop(0, 8, one, 0)


def residual_after(field, nu, turned, halo, force, partial, slopes, sides, out, cells, t):
    masks = residues()

    rows, inner = slice(8 * t, 8 * t + 8), slice(ROW0 + 8 * t, ROW0 + 8 * t + 8)

    def one(f, _):
        mu = nu[f, inner, :]
        for c in range(3):
            edges = Edges()
            high, low = halo[0, f, c], halo[1, f, c]
            for n in range(8):
                ahead = jnp.where(masks[(n + 7) % 8], high, turned[2, f, n, c, rows, :])
                behind = jnp.where(masks[n], low, turned[3, f, n, c, rows, :])
                slope = 0.5 * (ahead - behind)
                slopes[f, n, 2, c, rows, :] = slope
                if c == 2:
                    sides[0, f, n, rows, :] = ahead
                    sides[1, f, n, rows, :] = behind
                value = partial[f, n, c, rows, :] - force[f, n, c, rows, :]
                value = value + field[f, n, 2, inner, :] * slope - mu * (ahead + behind)
                out[f, n, c, inner, :] = value
                edges.add(masks, n, value)
            edges.store(cells, f, c)
        return 0

    lax.fori_loop(0, 2, one, 0)


def descent_before(field, res, nu, turned_u, turned, wrap, slopes, out):
    def one(step, _):
        f, t = step // 4, lax.rem(step, 4)
        rows, inner = tile(t), tile(t + 1)
        mus = nu.at[f, pl.ds(pl.multiple_of(8 * t, 8), 24)]
        mu, mu_up, mu_down = mus[8:16, :], mus[9:17, :], mus[7:15, :]
        for n in range(8):
            u1 = field.at[f, n, 1, pl.ds(pl.multiple_of(8 * t, 8), 24)]
            right0, left0 = 0.5 * turned_u[0, f, n, 0, rows, :], 0.5 * turned_u[1, f, n, 0, rows, :]
            up1, down1 = 0.5 * u1[9:17, :] + mu_up, 0.5 * u1[7:15, :] - mu_down
            centre = [res[f, n, e, inner, :] for e in range(3)]
            for c in range(3):
                r, view = centre[c], res.at[f, n, c, pl.ds(pl.multiple_of(8 * t, 8), 24)]
                right, left = turned[0, f, n, c, rows, :], turned[1, f, n, c, rows, :]
                ahead, behind = times(turned, wrap, f, n, c, rows)
                transport = centre[0] * slopes[f, n, c, 0, rows, :]
                transport = transport + centre[1] * slopes[f, n, c, 1, rows, :]
                transport = transport + centre[2] * slopes[f, n, c, 2, rows, :]
                flux = (right0 * right - left0 * left) + (up1 * view[9:17, :] - down1 * view[7:15, :])
                flux = flux + mu * ((right + left) - 6.0 * r)
                pull = (behind - ahead) + (r - res[1 - f, n, c, inner, :])
                descent = 0.5 * pull + (transport - flux)
                out[f, n, c, rows, :] = field[f, n, c, inner, :] - STEP * descent
        return 0

    lax.fori_loop(0, 8, one, 0)


def descent_after(nu, turned, halo, partial, sides, out, cells, t):
    masks = residues()

    rows, inner = slice(8 * t, 8 * t + 8), slice(ROW0 + 8 * t, ROW0 + 8 * t + 8)

    def one(f, _):
        mu = STEP * nu[f, inner, :]
        for c in range(3):
            edges = Edges()
            high, low = halo[0, f, c], halo[1, f, c]
            for n in range(8):
                ahead = jnp.where(masks[(n + 7) % 8], high, turned[2, f, n, c, rows, :])
                behind = jnp.where(masks[n], low, turned[3, f, n, c, rows, :])
                flux = sides[0, f, n, rows, :] * ahead - sides[1, f, n, rows, :] * behind
                value = partial[f, n, c, rows, :] + (0.5 * STEP * flux + mu * (ahead + behind))
                out[f, n, c, inner, :] = value
                if cells is not None:
                    edges.add(masks, n, value)
            if cells is not None:
                edges.store(cells, f, c)
        return 0

    lax.fori_loop(0, 2, one, 0)


def kernel(
    u_hbm, f_hbm, nu_in, out_r, out_u,
    raw_u, raw_f, pack_u, pack_f, field_a, field_b, force, res, partial, slopes, sides, nu,
    turned_u, turned_r, wrap, got_r, cells_out, cells_in, rows_out, rows_in, final,
    load_sem, self_sem, u_send, u_recv, f_send, f_recv, r_send, r_recv, o_send, o_recv,
    halo_send, halo_recv, nu_send, nu_recv,
):
    x, y, cls, z = position()
    xh = x // 2
    p = path_of(x, y)
    group = group_of(p, z)
    my_f, my_n = slot_of(x, y)
    rows = pl.ds(ROW0, 32)

    load_u = pltpu.make_async_copy(u_hbm, raw_u, load_sem.at[0])
    load_u.start()
    load_f = pltpu.make_async_copy(f_hbm, raw_f, load_sem.at[1])
    load_f.start()

    barrier = pltpu.get_barrier_semaphore()
    peers = [(lax.rem(x + dx, 4), lax.rem(y + dy, 4)) for dx, dy in OFFSETS]
    nx, ny, nz = along_path(p, z, 1)
    bx, by, bz = along_path(p, z, -1)
    ahead_dev, behind_dev = device_of(nx, ny, cls, nz), device_of(bx, by, cls, bz)
    other_core = device_of(x, y, 1 - cls, z)
    for px, py in peers:
        pl.semaphore_signal(barrier, inc=1, device_id=device_of(px, py, cls, z), device_id_type=MESH)
    for there in (
        other_core,
        device_of(x, y, cls, lax.rem(z + 1, 8)),
        device_of(x, y, cls, lax.rem(z + 7, 8)),
    ):
        pl.semaphore_signal(barrier, inc=1, device_id=there, device_id_type=MESH)

    row_id = lax.broadcasted_iota(jnp.int32, (8, 128), 0)
    for t in range(4):
        column = jnp.zeros((8, 128), jnp.float32)
        for s in range(8):
            r = 8 * t + s
            column = jnp.where(row_id == s, nu_in[r + xh * (31 - 2 * r)], column)
        nu[xh, ROW0 + 8 * t : ROW0 + 8 * t + 8, :] = column

    load_u.wait()
    pack(raw_u, pack_u, xh, my_n)
    pl.semaphore_wait(barrier, len(OFFSETS) + 3)

    def remote(src, dst, send, recv, there):
        return pltpu.make_async_remote_copy(
            src_ref=src, dst_ref=dst, send_sem=send, recv_sem=recv, device_id=there, device_id_type=MESH
        )

    pending = []
    u_in = []
    for j, (px, py) in enumerate(peers):
        copy = remote(
            pack_u.at[group_of(path_of(px, py), z)], field_a.at[my_f, my_n, :, rows],
            u_send.at[j], u_recv.at[j], device_of(px, py, cls, z),
        )
        copy.start()
        u_in.append(copy)
    own_u = pltpu.make_async_copy(pack_u.at[group], field_a.at[my_f, my_n, :, rows], self_sem.at[0])
    own_u.start()
    nu_copy = remote(nu.at[xh, rows], nu.at[xh, rows], nu_send, nu_recv, device_of(3 - x, y, cls, z))
    nu_copy.start()
    pending += u_in

    load_f.wait()
    pack(raw_f, pack_f, xh, my_n)
    f_in = []

    def send_force(h):
        half = pl.ds(16 * h, 16)
        for j, (px, py) in enumerate(peers):
            copy = remote(
                pack_f.at[group_of(path_of(px, py), z), :, half], force.at[my_f, my_n, :, half],
                f_send.at[h, j], f_recv.at[h, j], device_of(px, py, cls, z),
            )
            copy.start()
            f_in.append(copy)

    own_f = pltpu.make_async_copy(pack_f.at[group], force.at[my_f, my_n], self_sem.at[1])
    own_f.start()
    send_force(0)

    def send_cells(k, h):
        sends = [
            remote(
                cells_out.at[k, h, side], cells_in.at[k, h, side],
                halo_send.at[k, 2 * h + side], halo_recv.at[k, 2 * h + side], there,
            )
            for side, there in enumerate((behind_dev, ahead_dev))
        ]
        for copy in sends:
            copy.start()
        pending.extend(sends)
        return sends

    def send_rows(k, values):
        pack_rows(values, rows_out.at[k], final, cls)
        if k == 0:
            for f in range(2):
                edge = jnp.where(cls == 1, nu[f, ROW0 : ROW0 + 1, :], nu[f, ROW0 + 31 : ROW0 + 32, :])
                rows_out[k, f, 0, 3:4, :] = edge
        copy = remote(rows_out.at[k], rows_in.at[k], halo_send.at[k, 8], halo_recv.at[k, 8], other_core)
        copy.start()
        pending.append(copy)
        return copy

    def take_rows(k, values, copy):
        copy.wait_recv()
        fill_rows(values, rows_in.at[k], final, cls)
        if k == 0:
            for f in range(2):
                got = rows_in[k, f, 0, 3:4, :]
                fold = nu[1 - f, ROW0 + 31 : ROW0 + 32, :]
                nu[f, ROW0 - 1 : ROW0, :] = jnp.where(cls == 1, got, 0.0)
                nu[f, ROW0 + 32 : ROW0 + 33, :] = jnp.where(cls == 1, fold, got)

    def take_cells(sends):
        for copy in sends:
            copy.wait_recv()

    def residual_round(k, values, sends, last):
        edge = send_rows(k, values)
        rotate_all(values, turned_u, wrap)
        take_rows(k, values, edge)
        residual_before(values, nu, turned_u, wrap, slopes, partial)
        if not last:
            own_f.wait()
        nexts = []
        for h in range(4):
            take_cells(sends[h])
            if not last and h % 2 == 0:
                take_cells(f_in[15 * (h // 2) : 15 * (h // 2) + 15])
            residual_after(
                values, nu, turned_u, cells_in.at[k, h], force, partial, slopes, sides, res,
                cells_out.at[k + 1, h], h,
            )
            nexts.append(send_cells(k + 1, h))
        return nexts

    def descent_round(k, values, sends, out, last):
        edge = send_rows(k, res)
        rotate_all(res, turned_r, wrap)
        take_rows(k, res, edge)
        descent_before(values, res, nu, turned_u, turned_r, wrap, slopes, partial)
        nexts = []
        for h in range(4):
            take_cells(sends[h])
            descent_after(
                nu, turned_r, cells_in.at[k, h], partial, sides, out,
                None if last else cells_out.at[k + 1, h], h,
            )
            if not last:
                nexts.append(send_cells(k + 1, h))
        return nexts

    def send_back(values, dst, send, recv):
        copies = []
        for j, (px, py) in enumerate(peers):
            f, n = slot_of(px, py)
            copy = remote(
                values.at[f, n, :, rows], dst.at[group], send.at[j], recv.at[j], device_of(px, py, cls, z)
            )
            copy.start()
            copies.append(copy)
        return copies

    nu_copy.wait()
    own_u.wait()
    take_cells(u_in)

    sends = []
    for h in range(4):
        pack_cells(field_a, cells_out.at[0, h], h)
        sends.append(send_cells(0, h))
    send_force(1)
    sends = residual_round(0, field_a, sends, False)
    pending += f_in
    sends = descent_round(1, field_a, sends, field_b, False)
    sends = residual_round(2, field_b, sends, True)

    r_out = send_back(res, got_r, r_send, r_recv)
    own_r = pltpu.make_async_copy(res.at[my_f, my_n, :, rows], got_r.at[group], self_sem.at[2])
    own_r.start()
    descent_round(3, field_b, sends, field_a, True)
    o_out = send_back(field_a, out_u, o_send, o_recv)
    own_o = pltpu.make_async_copy(field_a.at[my_f, my_n, :, rows], out_u.at[group], self_sem.at[3])
    own_o.start()

    own_r.wait()
    take_cells(r_out)
    unpack(got_r, raw_u, xh, my_n)
    store_r = pltpu.make_async_copy(raw_u, out_r, load_sem.at[0])
    store_r.start()
    for copy in pending + r_out:
        copy.wait_send()
    store_r.wait()
    own_o.wait()
    for copy in o_out:
        copy.wait()


def finish(u_hbm, r_hbm, u_out, r_out, packed, plain, passed, u_load, u_store, r_sem):
    x, y, _, _ = position()
    xh = x // 2
    _, n = slot_of(x, y)
    loads, stores = [], []
    for t in range(4):
        here, there = tile(t), tile(t + xh * (3 - 2 * t))
        loads.append(pltpu.make_async_copy(u_hbm.at[:, :, there], packed.at[:, :, there], u_load.at[t]))
        stores.append(pltpu.make_async_copy(plain.at[:, :, here], u_out.at[:, :, here], u_store.at[t]))
        loads[-1].start()
    through = pltpu.make_async_copy(r_hbm, passed, r_sem.at[0])
    through.start()
    for t in range(4):
        loads[t].wait()
        unpack_rows(packed, plain, xh, n, t)
        stores[t].start()
        if t == 0:
            through.wait()
            onward = pltpu.make_async_copy(passed, r_out, r_sem.at[1])
            onward.start()
    for copy in stores + [onward]:
        copy.wait()


def local(starting_speed_vector, driving_source, viscosity):
    block = starting_speed_vector.shape
    f32 = jnp.float32
    flat = (3, 16, 32, 128)
    plain, packed = pltpu.VMEM(flat, f32), pltpu.VMEM((16, 3, 32, 128), f32)
    slabs, padded = pltpu.VMEM((2, 8, 3, 32, 128), f32), pltpu.VMEM((2, 8, 3, 48, 128), f32)
    turned = pltpu.VMEM((4, 2, 8, 3, 32, 128), f32)
    cells = pltpu.VMEM((4, 4, 2, 2, 3, 8, 128), f32)
    edge = pltpu.VMEM((4, 2, 8, 8, 128), f32)
    dma = pltpu.SemaphoreType.DMA
    anywhere = pl.BlockSpec(memory_space=pl.ANY)
    got_r, got_u = pl.pallas_call(
        kernel,
        out_shape=(jax.ShapeDtypeStruct(flat, f32), jax.ShapeDtypeStruct((16, 3, 32, 128), f32)),
        in_specs=[anywhere, anywhere, pl.BlockSpec(memory_space=pltpu.SMEM)],
        out_specs=(anywhere, anywhere),
        scratch_shapes=[
            plain, plain, packed, packed, padded, padded, slabs, padded, slabs,
            pltpu.VMEM((2, 8, 3, 3, 32, 128), f32),
            pltpu.VMEM((2, 2, 8, 32, 128), f32),
            pltpu.VMEM((2, 48, 128), f32),
            turned, turned,
            pltpu.VMEM((2, 2, 3, 32, 128), f32),
            packed, cells, cells, edge, edge,
            pltpu.VMEM((2, 8, 8, 128), f32),
            dma((2,)), dma((4,)),
            dma((15,)), dma((15,)), dma((2, 15)), dma((2, 15)),
            dma((15,)), dma((15,)), dma((15,)), dma((15,)),
            dma((4, 9)), dma((4, 9)), dma(()), dma(()),
        ],
        compiler_params=pltpu.CompilerParams(collective_id=0, has_side_effects=True),
        name="descend",
    )(starting_speed_vector.reshape(flat), driving_source.reshape(flat), viscosity)
    orbit, residual = pl.pallas_call(
        finish,
        out_shape=(jax.ShapeDtypeStruct(flat, f32), jax.ShapeDtypeStruct(flat, f32)),
        in_specs=[anywhere, anywhere],
        out_specs=(anywhere, anywhere),
        scratch_shapes=[packed, plain, plain, dma((4,)), dma((4,)), dma((2,))],
        name="finish",
    )(got_u, got_r)
    return orbit.reshape(block), residual.reshape(block)


def solution(mesh):
    spec = P(None, "tm", None, "wall", "span")
    return jax.shard_map(
        local, mesh=mesh, in_specs=(spec, spec, P("wall")), out_specs=(spec, spec), check_vma=False
    )
```

```python
import jax
import jax.numpy as jnp
from jax import lax
from jax.experimental import pallas as pl
from jax.experimental.pallas import tpu as pltpu
from jax.sharding import PartitionSpec as P

STEP = 0.05
SIGN = (1.0, -1.0, 1.0)
MESH = pl.DeviceIdType.MESH
OFFSETS = sorted(
    ((dx, dy) for dx in range(4) for dy in range(4) if (dx, dy) != (0, 0)),
    key=lambda o: -(min(o[0], 4 - o[0]) + min(o[1], 4 - o[1])),
)
ROW0 = 8


def roll(v, shift, axis=1):
    return pltpu.roll(v, shift % 128 if isinstance(shift, int) else shift, axis)


def device_of(x, y, cls, z):
    xh, xl = x // 2, lax.rem(x, 2)
    return (xl * 4 + y, xh * 2 + (cls + xh - 2 * cls * xh), z)


def position():
    tm, wall, z = lax.axis_index("tm"), lax.axis_index("wall"), lax.axis_index("span")
    xl, y, xh, core = tm // 4, lax.rem(tm, 4), wall // 2, lax.rem(wall, 2)
    return xh * 2 + xl, y, core + xh - 2 * core * xh, z


def path_of(x, y):
    odd = lax.rem(y, 2)
    return 4 * y + x + odd * (3 - 2 * x)


def chip_at(p):
    y, a = p // 4, lax.rem(p, 4)
    odd = lax.rem(y, 2)
    return a + odd * (3 - 2 * a), y


def group_of(p, z):
    return p + lax.rem(z, 2) * (15 - 2 * p)


def slot_of(x, y):
    xh, xl = x // 2, lax.rem(x, 2)
    return xh, lax.rem(4 * xl + y + 4 * xh, 8)


def along_path(p, z, way):
    there = p + way * (1 - 2 * lax.rem(z, 2))
    over = (there + 16) // 16 - 1
    over = over * over
    x, y = chip_at(there * (1 - over) + p * over)
    return x, y, lax.rem(z + way * over + 8, 8)


def swap_groups(ins, before=0, after=0):
    lane = lax.broadcasted_iota(jnp.int32, (8, 128), 1)
    turned = [roll(v, lax.rem(8 * i + before + 128, 128)) for i, v in enumerate(ins)]
    mixed = [turned[-d % 16] for d in range(16)]
    for bit in range(4):
        mask = (lane & (8 << bit)) != 0
        mixed = [jnp.where(mask, mixed[(d - (1 << bit)) % 16], mixed[d]) for d in range(16)]
    return [roll(v, lax.rem(128 - 8 * d + after, 128)) for d, v in enumerate(mixed)]


def frame_rows(v, xh):
    row = lax.broadcasted_iota(jnp.int32, (8, 128), 0)
    return jnp.take_along_axis(v, row + xh * (7 - 2 * row), axis=0, mode="promise_in_bounds")


def frame_sign(v, c, xh):
    return v * (1.0 - 2.0 * xh.astype(jnp.float32)) if SIGN[c] < 0 else v


def tile(t):
    return pl.ds(pl.multiple_of(8 * t, 8), 8)


def pack(src, dst, xh, n):
    def one(t, _):
        to = tile(t + xh * (3 - 2 * t))
        for c in range(3):
            ins = [src[c, i, tile(t), :] for i in range(16)]
            for d, v in enumerate(swap_groups(ins, 0, n)):
                dst[d, c, to, :] = frame_sign(frame_rows(v, xh), c, xh)
        return 0

    lax.fori_loop(0, 4, one, 0)


def unpack_rows(src, dst, xh, n, t):
    to = tile(t + xh * (3 - 2 * t))
    for c in range(3):
        ins = [src[d, c, to, :] for d in range(16)]
        for i, v in enumerate(swap_groups(ins, -n, 0)):
            dst[c, i, tile(t), :] = frame_sign(frame_rows(v, xh), c, xh)


def unpack(src, dst, xh, n):
    def one(t, _):
        unpack_rows(src, dst, xh, n, t)
        return 0

    lax.fori_loop(0, 4, one, 0)


def residues():
    lane = lax.broadcasted_iota(jnp.int32, (8, 128), 1) & 7
    return [lane == q for q in range(8)]


class Edges:
    def __init__(self):
        self.first = self.last = None

    def add(self, masks, n, v):
        self.first = v if n == 0 else jnp.where(masks[n], v, self.first)
        self.last = v if n == 0 else jnp.where(masks[(n + 7) % 8], v, self.last)

    def store(self, out, f, c):
        out[0, f, c] = roll(self.first, 7)
        out[1, f, c] = roll(self.last, -7)


def pack_cells(field, out, t):
    masks = residues()

    def one(f, _):
        for c in range(3):
            edges = Edges()
            for n in range(8):
                edges.add(masks, n, field[f, n, c, ROW0 + 8 * t : ROW0 + 8 * t + 8, :])
            edges.store(out, f, c)
        return 0

    one(0, 0)
    one(1, 0)


def pack_rows(field, edge, final, cls):
    for f in range(2):
        for n in range(8):
            for c in range(3):
                first = field[f, n, c, ROW0 : ROW0 + 1, :]
                last = field[f, n, c, ROW0 + 31 : ROW0 + 32, :]
                edge[f, n, c : c + 1, :] = jnp.where(cls == 1, first, last)
                final[f, n, c : c + 1, :] = last


def fill_rows(field, edge, final, cls):
    row = lax.broadcasted_iota(jnp.int32, (8, 128), 0)
    sign = jnp.where(row == 1, SIGN[1], 1.0)
    for f in range(2):
        for n in range(8):
            got = edge[f, n]
            fold = sign * roll(final[1 - f, (n + 4) % 8], -4 if n < 4 else 4)
            low = jnp.where(cls == 1, got, 0.0)
            high = jnp.where(cls == 1, fold, got)
            for c in range(3):
                field[f, n, c, ROW0 - 1 : ROW0, :] = low[c : c + 1, :]
                field[f, n, c, ROW0 + 32 : ROW0 + 33, :] = high[c : c + 1, :]


def rotate_all(field, turned, wrap):
    def one(f, _):
        for c in range(3):
            for t in range(4):
                rows, out = slice(ROW0 + 8 * t, ROW0 + 8 * t + 8), slice(8 * t, 8 * t + 8)
                for n in range(8):
                    v = field[f, n, c, rows, :]
                    for kind, shift in enumerate((-8, 8, -1, 1)):
                        turned[kind, f, n, c, out, :] = roll(v, shift)
                    if n == 0:
                        wrap[0, f, c, out, :] = roll(v, 7)
                    if n == 7:
                        wrap[1, f, c, out, :] = roll(v, -7)
        return 0

    one(0, 0)
    one(1, 0)


def times(turned, wrap, f, n, c, rows):
    ahead = wrap[0, f, c, rows, :] if n == 7 else turned[2, f, n + 1, c, rows, :]
    behind = wrap[1, f, c, rows, :] if n == 0 else turned[3, f, n - 1, c, rows, :]
    return ahead, behind


def residual_before(field, nu, turned, wrap, slopes, out):
    def one(step, _):
        f, t = step // 4, lax.rem(step, 4)
        rows = tile(t)
        mu = nu[f, tile(t + 1), :]
        for n in range(8):
            view = [field.at[f, n, c, pl.ds(pl.multiple_of(8 * t, 8), 24)] for c in range(3)]
            u0, u1 = view[0][8:16, :], view[1][8:16, :]
            for c in range(3):
                v, up, down = view[c][8:16, :], view[c][9:17, :], view[c][7:15, :]
                right, left = turned[0, f, n, c, rows, :], turned[1, f, n, c, rows, :]
                ahead, behind = times(turned, wrap, f, n, c, rows)
                along = 0.5 * (right - left)
                across = 0.5 * (up - down)
                slopes[f, n, 0, c, rows, :] = along
                slopes[f, n, 1, c, rows, :] = across
                lap = (right + left) + (up + down) - 6.0 * v
                pull = (ahead - behind) + (v - field[1 - f, n, c, tile(t + 1), :])
                out[f, n, c, rows, :] = 0.5 * pull + (u0 * along + u1 * across) - mu * lap
        return 0

    lax.fori_loop(0, 8, one, 0)


def residual_after(field, nu, turned, halo, force, partial, slopes, sides, out, cells, t):
    masks = residues()

    rows, inner = slice(8 * t, 8 * t + 8), slice(ROW0 + 8 * t, ROW0 + 8 * t + 8)

    def one(f, _):
        mu = nu[f, inner, :]
        for c in range(3):
            edges = Edges()
            high, low = halo[0, f, c], halo[1, f, c]
            for n in range(8):
                ahead = jnp.where(masks[(n + 7) % 8], high, turned[2, f, n, c, rows, :])
                behind = jnp.where(masks[n], low, turned[3, f, n, c, rows, :])
                slope = 0.5 * (ahead - behind)
                slopes[f, n, 2, c, rows, :] = slope
                if c == 2:
                    sides[0, f, n, rows, :] = ahead
                    sides[1, f, n, rows, :] = behind
                value = partial[f, n, c, rows, :] - force[f, n, c, rows, :]
                value = value + field[f, n, 2, inner, :] * slope - mu * (ahead + behind)
                out[f, n, c, inner, :] = value
                edges.add(masks, n, value)
            edges.store(cells, f, c)
        return 0

    one(0, 0)
    one(1, 0)


def descent_before(field, res, nu, turned_u, turned, wrap, slopes, out):
    def one(step, _):
        f, t = step // 4, lax.rem(step, 4)
        rows, inner = tile(t), tile(t + 1)
        mus = nu.at[f, pl.ds(pl.multiple_of(8 * t, 8), 24)]
        mu, mu_up, mu_down = mus[8:16, :], mus[9:17, :], mus[7:15, :]
        for n in range(8):
            u1 = field.at[f, n, 1, pl.ds(pl.multiple_of(8 * t, 8), 24)]
            right0, left0 = 0.5 * turned_u[0, f, n, 0, rows, :], 0.5 * turned_u[1, f, n, 0, rows, :]
            up1, down1 = 0.5 * u1[9:17, :] + mu_up, 0.5 * u1[7:15, :] - mu_down
            centre = [res[f, n, e, inner, :] for e in range(3)]
            for c in range(3):
                r, view = centre[c], res.at[f, n, c, pl.ds(pl.multiple_of(8 * t, 8), 24)]
                right, left = turned[0, f, n, c, rows, :], turned[1, f, n, c, rows, :]
                ahead, behind = times(turned, wrap, f, n, c, rows)
                transport = centre[0] * slopes[f, n, c, 0, rows, :]
                transport = transport + centre[1] * slopes[f, n, c, 1, rows, :]
                transport = transport + centre[2] * slopes[f, n, c, 2, rows, :]
                flux = (right0 * right - left0 * left) + (up1 * view[9:17, :] - down1 * view[7:15, :])
                flux = flux + mu * ((right + left) - 6.0 * r)
                pull = (behind - ahead) + (r - res[1 - f, n, c, inner, :])
                descent = 0.5 * pull + (transport - flux)
                out[f, n, c, rows, :] = field[f, n, c, inner, :] - STEP * descent
        return 0

    lax.fori_loop(0, 8, one, 0)


def descent_after(nu, turned, halo, partial, sides, out, cells, t):
    masks = residues()

    rows, inner = slice(8 * t, 8 * t + 8), slice(ROW0 + 8 * t, ROW0 + 8 * t + 8)

    def one(f, _):
        mu = STEP * nu[f, inner, :]
        for c in range(3):
            edges = Edges()
            high, low = halo[0, f, c], halo[1, f, c]
            for n in range(8):
                ahead = jnp.where(masks[(n + 7) % 8], high, turned[2, f, n, c, rows, :])
                behind = jnp.where(masks[n], low, turned[3, f, n, c, rows, :])
                flux = sides[0, f, n, rows, :] * ahead - sides[1, f, n, rows, :] * behind
                value = partial[f, n, c, rows, :] + (0.5 * STEP * flux + mu * (ahead + behind))
                out[f, n, c, inner, :] = value
                if cells is not None:
                    edges.add(masks, n, value)
            if cells is not None:
                edges.store(cells, f, c)
        return 0

    one(0, 0)
    one(1, 0)


def kernel(
    u_hbm, f_hbm, nu_in, out_r, out_u,
    raw_u, raw_f, pack_u, pack_f, field_a, field_b, force, res, partial, slopes, sides, nu,
    turned_u, turned_r, wrap, got_r, cells_out, cells_in, rows_out, rows_in, final,
    load_sem, self_sem, u_send, u_recv, f_send, f_recv, r_send, r_recv, o_send, o_recv,
    halo_send, halo_recv, nu_send, nu_recv,
):
    x, y, cls, z = position()
    xh = x // 2
    p = path_of(x, y)
    group = group_of(p, z)
    my_f, my_n = slot_of(x, y)
    rows = pl.ds(ROW0, 32)

    load_u = pltpu.make_async_copy(u_hbm, raw_u, load_sem.at[0])
    load_u.start()
    load_f = pltpu.make_async_copy(f_hbm, raw_f, load_sem.at[1])
    load_f.start()

    barrier = pltpu.get_barrier_semaphore()
    peers = [(lax.rem(x + dx, 4), lax.rem(y + dy, 4)) for dx, dy in OFFSETS]
    nx, ny, nz = along_path(p, z, 1)
    bx, by, bz = along_path(p, z, -1)
    ahead_dev, behind_dev = device_of(nx, ny, cls, nz), device_of(bx, by, cls, bz)
    other_core = device_of(x, y, 1 - cls, z)
    for px, py in peers:
        pl.semaphore_signal(barrier, inc=1, device_id=device_of(px, py, cls, z), device_id_type=MESH)
    for there in (
        other_core,
        device_of(x, y, cls, lax.rem(z + 1, 8)),
        device_of(x, y, cls, lax.rem(z + 7, 8)),
    ):
        pl.semaphore_signal(barrier, inc=1, device_id=there, device_id_type=MESH)

    row_id = lax.broadcasted_iota(jnp.int32, (8, 128), 0)
    for t in range(4):
        column = jnp.zeros((8, 128), jnp.float32)
        for s in range(8):
            r = 8 * t + s
            column = jnp.where(row_id == s, nu_in[r + xh * (31 - 2 * r)], column)
        nu[xh, ROW0 + 8 * t : ROW0 + 8 * t + 8, :] = column

    load_u.wait()
    pack(raw_u, pack_u, xh, my_n)
    pl.semaphore_wait(barrier, len(OFFSETS) + 3)

    def remote(src, dst, send, recv, there):
        return pltpu.make_async_remote_copy(
            src_ref=src, dst_ref=dst, send_sem=send, recv_sem=recv, device_id=there, device_id_type=MESH
        )

    pending = []
    u_in = []
    for j, (px, py) in enumerate(peers):
        copy = remote(
            pack_u.at[group_of(path_of(px, py), z)], field_a.at[my_f, my_n, :, rows],
            u_send.at[j], u_recv.at[j], device_of(px, py, cls, z),
        )
        copy.start()
        u_in.append(copy)
    own_u = pltpu.make_async_copy(pack_u.at[group], field_a.at[my_f, my_n, :, rows], self_sem.at[0])
    own_u.start()
    nu_copy = remote(nu.at[xh, rows], nu.at[xh, rows], nu_send, nu_recv, device_of(3 - x, y, cls, z))
    nu_copy.start()
    pending += u_in

    load_f.wait()
    pack(raw_f, pack_f, xh, my_n)
    f_in = []

    def send_force(h):
        half = pl.ds(16 * h, 16)
        for j, (px, py) in enumerate(peers):
            copy = remote(
                pack_f.at[group_of(path_of(px, py), z), :, half], force.at[my_f, my_n, :, half],
                f_send.at[h, j], f_recv.at[h, j], device_of(px, py, cls, z),
            )
            copy.start()
            f_in.append(copy)

    own_f = pltpu.make_async_copy(pack_f.at[group], force.at[my_f, my_n], self_sem.at[1])
    own_f.start()
    send_force(0)

    def send_cells(k, h):
        sends = [
            remote(
                cells_out.at[k, h, side], cells_in.at[k, h, side],
                halo_send.at[k, 2 * h + side], halo_recv.at[k, 2 * h + side], there,
            )
            for side, there in enumerate((behind_dev, ahead_dev))
        ]
        for copy in sends:
            copy.start()
        pending.extend(sends)
        return sends

    def send_rows(k, values):
        pack_rows(values, rows_out.at[k], final, cls)
        if k == 0:
            for f in range(2):
                edge = jnp.where(cls == 1, nu[f, ROW0 : ROW0 + 1, :], nu[f, ROW0 + 31 : ROW0 + 32, :])
                rows_out[k, f, 0, 3:4, :] = edge
        copy = remote(rows_out.at[k], rows_in.at[k], halo_send.at[k, 8], halo_recv.at[k, 8], other_core)
        copy.start()
        pending.append(copy)
        return copy

    def take_rows(k, values, copy):
        copy.wait_recv()
        fill_rows(values, rows_in.at[k], final, cls)
        if k == 0:
            for f in range(2):
                got = rows_in[k, f, 0, 3:4, :]
                fold = nu[1 - f, ROW0 + 31 : ROW0 + 32, :]
                nu[f, ROW0 - 1 : ROW0, :] = jnp.where(cls == 1, got, 0.0)
                nu[f, ROW0 + 32 : ROW0 + 33, :] = jnp.where(cls == 1, fold, got)

    def take_cells(sends):
        for copy in sends:
            copy.wait_recv()

    def residual_round(k, values, sends, last):
        edge = send_rows(k, values)
        rotate_all(values, turned_u, wrap)
        take_rows(k, values, edge)
        residual_before(values, nu, turned_u, wrap, slopes, partial)
        if not last:
            own_f.wait()
        nexts = []
        for h in range(4):
            take_cells(sends[h])
            if not last and h % 2 == 0:
                take_cells(f_in[15 * (h // 2) : 15 * (h // 2) + 15])
            residual_after(
                values, nu, turned_u, cells_in.at[k, h], force, partial, slopes, sides, res,
                cells_out.at[k + 1, h], h,
            )
            nexts.append(send_cells(k + 1, h))
        return nexts

    def descent_round(k, values, sends, out, last):
        edge = send_rows(k, res)
        rotate_all(res, turned_r, wrap)
        take_rows(k, res, edge)
        descent_before(values, res, nu, turned_u, turned_r, wrap, slopes, partial)
        nexts = []
        for h in range(4):
            take_cells(sends[h])
            descent_after(
                nu, turned_r, cells_in.at[k, h], partial, sides, out,
                None if last else cells_out.at[k + 1, h], h,
            )
            if not last:
                nexts.append(send_cells(k + 1, h))
        return nexts

    def send_back(values, dst, send, recv):
        copies = []
        for j, (px, py) in enumerate(peers):
            f, n = slot_of(px, py)
            copy = remote(
                values.at[f, n, :, rows], dst.at[group], send.at[j], recv.at[j], device_of(px, py, cls, z)
            )
            copy.start()
            copies.append(copy)
        return copies

    nu_copy.wait()
    own_u.wait()
    take_cells(u_in)

    sends = []
    for h in range(4):
        pack_cells(field_a, cells_out.at[0, h], h)
        sends.append(send_cells(0, h))
    send_force(1)
    sends = residual_round(0, field_a, sends, False)
    pending += f_in
    sends = descent_round(1, field_a, sends, field_b, False)
    sends = residual_round(2, field_b, sends, True)

    r_out = send_back(res, got_r, r_send, r_recv)
    own_r = pltpu.make_async_copy(res.at[my_f, my_n, :, rows], got_r.at[group], self_sem.at[2])
    own_r.start()
    descent_round(3, field_b, sends, field_a, True)
    o_out = send_back(field_a, out_u, o_send, o_recv)
    own_o = pltpu.make_async_copy(field_a.at[my_f, my_n, :, rows], out_u.at[group], self_sem.at[3])
    own_o.start()

    own_r.wait()
    take_cells(r_out)
    unpack(got_r, raw_u, xh, my_n)
    store_r = pltpu.make_async_copy(raw_u, out_r, load_sem.at[0])
    store_r.start()
    for copy in pending + r_out:
        copy.wait_send()
    store_r.wait()
    own_o.wait()
    for copy in o_out:
        copy.wait()


def finish(u_hbm, r_hbm, u_out, r_out, packed, plain, passed, u_load, u_store, r_sem):
    x, y, _, _ = position()
    xh = x // 2
    _, n = slot_of(x, y)
    loads, stores = [], []
    for t in range(4):
        here, there = tile(t), tile(t + xh * (3 - 2 * t))
        loads.append(pltpu.make_async_copy(u_hbm.at[:, :, there], packed.at[:, :, there], u_load.at[t]))
        stores.append(pltpu.make_async_copy(plain.at[:, :, here], u_out.at[:, :, here], u_store.at[t]))
        loads[-1].start()
        if t == 0:
            through = pltpu.make_async_copy(r_hbm, passed, r_sem.at[0])
            through.start()
    for t in range(4):
        loads[t].wait()
        unpack_rows(packed, plain, xh, n, t)
        stores[t].start()
        if t == 0:
            through.wait()
            onward = pltpu.make_async_copy(passed, r_out, r_sem.at[1])
            onward.start()
    for copy in stores + [onward]:
        copy.wait()


def local(starting_speed_vector, driving_source, viscosity):
    block = starting_speed_vector.shape
    f32 = jnp.float32
    flat = (3, 16, 32, 128)
    plain, packed = pltpu.VMEM(flat, f32), pltpu.VMEM((16, 3, 32, 128), f32)
    slabs, padded = pltpu.VMEM((2, 8, 3, 32, 128), f32), pltpu.VMEM((2, 8, 3, 48, 128), f32)
    turned = pltpu.VMEM((4, 2, 8, 3, 32, 128), f32)
    cells = pltpu.VMEM((4, 4, 2, 2, 3, 8, 128), f32)
    edge = pltpu.VMEM((4, 2, 8, 8, 128), f32)
    dma = pltpu.SemaphoreType.DMA
    anywhere = pl.BlockSpec(memory_space=pl.ANY)
    got_r, got_u = pl.pallas_call(
        kernel,
        out_shape=(jax.ShapeDtypeStruct(flat, f32), jax.ShapeDtypeStruct((16, 3, 32, 128), f32)),
        in_specs=[anywhere, anywhere, pl.BlockSpec(memory_space=pltpu.SMEM)],
        out_specs=(anywhere, anywhere),
        scratch_shapes=[
            plain, plain, packed, packed, padded, padded, slabs, padded, slabs,
            pltpu.VMEM((2, 8, 3, 3, 32, 128), f32),
            pltpu.VMEM((2, 2, 8, 32, 128), f32),
            pltpu.VMEM((2, 48, 128), f32),
            turned, turned,
            pltpu.VMEM((2, 2, 3, 32, 128), f32),
            packed, cells, cells, edge, edge,
            pltpu.VMEM((2, 8, 8, 128), f32),
            dma((2,)), dma((4,)),
            dma((15,)), dma((15,)), dma((2, 15)), dma((2, 15)),
            dma((15,)), dma((15,)), dma((15,)), dma((15,)),
            dma((4, 9)), dma((4, 9)), dma(()), dma(()),
        ],
        compiler_params=pltpu.CompilerParams(collective_id=0, has_side_effects=True),
        name="descend",
    )(starting_speed_vector.reshape(flat), driving_source.reshape(flat), viscosity)
    orbit, residual = pl.pallas_call(
        finish,
        out_shape=(jax.ShapeDtypeStruct(flat, f32), jax.ShapeDtypeStruct(flat, f32)),
        in_specs=[anywhere, anywhere],
        out_specs=(anywhere, anywhere),
        scratch_shapes=[packed, plain, plain, dma((4,)), dma((4,)), dma((2,))],
        name="finish",
    )(got_u, got_r)
    return orbit.reshape(block), residual.reshape(block)


def solution(mesh):
    spec = P(None, "tm", None, "wall", "span")
    return jax.shard_map(
        local, mesh=mesh, in_specs=(spec, spec, P("wall")), out_specs=(spec, spec), check_vma=False
    )
```
